32 devices in a mesh: mem: 4 (over x, core), tile: 8 (over z, y).
Axes of the slice: x: 2, y: 2, z: 4, core: 2. Of those that a mesh axis runs over, the one named last changes fastest.
Arguments:
- perturbations: bfloat16 [8, 32, 2, 64, 3072], P('mem', None, None, 'tile'), may hold values from -6 to 6
- gradient: bfloat16 [32, 2, 64, 3072], P('mem', None, 'tile'), may hold values from -6 to 6
- static_variance: float32 [32, 2, 64, 3072], P('mem', None, 'tile'), may hold values from 0.05 to 0.5
- level_steps: int32 [32], replicated, may hold values from 1 to 10, as said below
- class_map: int32 [64, 3072], replicated, may hold values from 0 to 3
- class_diffusivity: float32 [4], replicated, may hold values from 0.05 to 0.35
Outputs:
- increment: float32 [32, 2, 64, 3072], P('mem', None, 'tile')
The draws below stay inside these ranges and needn't reach their ends.
Inputs may be any that keep to these rules, and one draw needn't show every extreme that they name: `level_steps`: each level's number of diffusion steps; some level takes exactly 10.
All inputs are finite; a program needn't handle non-finite values.
Results may differ from the reference program's by a relative error of at most 0.0021.
Values may be sent and summed in bfloat16 or wider, within the bound.
No kernel may reach another device: no remote copies, remote signals or barrier semaphores. Data moves between devices by JAX's collectives and lax.ppermute only.
A program may use at most 128 MiB of HBM per device.

```python
import math
import jax
import jax.numpy as jnp
from jax import lax

LEV = 32
NLON = 3072
ITERS = 10
NCLASS = 4
MEMBERS = 8
NLAT = 64


def draw_level_steps(key, part):
    band = max(LEV // 8, 1)
    keys = jax.random.split(jax.random.fold_in(key, 31), 4)
    start = jax.random.randint(keys[0], (), 0, LEV - band + 1)
    shallow = jax.random.randint(keys[1], (LEV,), 1, 4)
    deep = jax.random.randint(keys[2], (LEV,), ITERS // 2 + 1, ITERS + 1)
    level_index = jnp.arange(LEV, dtype=jnp.int32)
    inside = (level_index >= start) & (level_index < start + band)
    steps = jnp.where(inside, deep, shallow)
    peak = start + jax.random.randint(keys[3], (), 0, band)
    steps = jnp.where(level_index == peak, ITERS, steps)
    return steps.astype(jnp.int32)


def touch_ends(values, key, low, high):
    spot = [jax.random.randint(jax.random.fold_in(key, axis), (), 0, length) for axis, length in enumerate(values.shape)]
    longest = values.shape.index(max(values.shape))
    next_to = spot[:longest] + [(spot[longest] + 1) % values.shape[longest]] + spot[longest + 1:]
    return values.at[tuple(spot)].set(low).at[tuple(next_to)].set(high)


def block_levels(stream_key, dims, cuts, smallest, largest):
    def one(position, parts):
        draws = jax.random.uniform(jax.random.fold_in(jax.random.fold_in(stream_key, 6), position), (parts,), jnp.float32, smallest / len(cuts), largest / len(cuts))
        return jnp.repeat(jnp.exp(draws), dims[position] // parts).reshape((-1,) + (1,) * (len(dims) - position - 1))

    factor_of = one(*cuts[0])
    for cut in cuts[1:]:
        factor_of = factor_of * one(*cut)
    return factor_of


def centred(own_key, dims, deviation, reach, cuts=(), kind=jnp.bfloat16):
    drawn = jax.random.normal(own_key, dims, jnp.float32) * deviation
    if len(cuts) > 0:
        drawn = block_levels(own_key, dims, cuts, -0.22, 0.18) * drawn
    return jnp.clip(drawn, min=-reach, max=reach).astype(kind)


def setup_inputs(seed: int = 0) -> dict:
    streams_of = jax.random.split(jax.random.key(seed), 7)
    perturbations = centred(streams_of[0], (MEMBERS, LEV, 2, NLAT, NLON), 1.0, 6.0, ((0, 4), (3, 8)))
    gradient = centred(streams_of[1], (LEV, 2, NLAT, NLON), 1.0, 6.0, ((0, 4), (2, 8)))
    static_variance = jnp.clip(jnp.exp(math.log(0.5) - 2.3025851 * jax.random.uniform(streams_of[2], (LEV, 2, NLAT, NLON), jnp.float32) ** block_levels(streams_of[2], (LEV, 2, NLAT, NLON), ((0, 4), (2, 8)), -0.2, 0.2)), 0.05, 0.5)
    level_steps = draw_level_steps(jax.random.fold_in(streams_of[6], 71), 0)
    class_map = touch_ends(jax.random.randint(streams_of[4], (NLAT, NLON), 0, NCLASS), jax.random.fold_in(streams_of[4], 1), 0, NCLASS - 1).astype(jnp.int32)
    class_diffusivity = jnp.clip(jnp.exp(jax.random.uniform(streams_of[5], (NCLASS,), jnp.float32, math.log(0.05), math.log(0.35))), 0.05, 0.35)
    return dict(perturbations=perturbations, gradient=gradient, static_variance=static_variance, level_steps=level_steps, class_map=class_map, class_diffusivity=class_diffusivity)


def diffusivity_field(class_map, class_diffusivity):
    classes = jnp.arange(NCLASS, dtype=jnp.int32)
    match = (class_map[None, :, :] == classes[:, None, None]).astype(jnp.float32)
    return jnp.sum(match * class_diffusivity[:, None, None], axis=0)


def diffusion_step(field, diffusivity):
    zero_row = jnp.zeros_like(field[:1])
    northern = jnp.concatenate([zero_row, field[:-1]], axis=0)
    southern = jnp.concatenate([field[1:], zero_row], axis=0)
    eastern = jnp.roll(field, -1, axis=1)
    western = jnp.roll(field, 1, axis=1)
    corners = jnp.roll(northern, -1, axis=1) + jnp.roll(northern, 1, axis=1)
    corners = corners + jnp.roll(southern, -1, axis=1) + jnp.roll(southern, 1, axis=1)
    laplace = (4.0 * (northern + southern + eastern + western) + corners - 20.0 * field) / 6.0
    return field + diffusivity * laplace


def diffuse(field, steps, diffusivity):
    return lax.fori_loop(jnp.int32(0), steps.astype(jnp.int32), lambda step_index, state: diffusion_step(state, diffusivity), field)


def reference(perturbations, gradient, static_variance, level_steps, class_map, class_diffusivity):
    diffusivity = diffusivity_field(class_map, class_diffusivity)
    grad_float = gradient.astype(jnp.float32)

    def add_member(running, member_data):
        member_float = member_data.astype(jnp.float32)
        product = jnp.sum(member_float * grad_float, axis=1).astype(jnp.bfloat16)

        def smooth_one(packed):
            return diffuse(packed[0].astype(jnp.float32), packed[1], diffusivity).astype(jnp.bfloat16)

        smooth = lax.map(smooth_one, (product, level_steps))
        return running + member_float * smooth.astype(jnp.float32)[:, None], None

    start = jnp.zeros(gradient.shape, jnp.float32)
    ensemble, unused = lax.scan(add_member, start, perturbations)
    return static_variance * grad_float + ensemble
```

```python
import functools
import jax
import jax.numpy as jnp
from jax import lax
from jax.experimental import pallas as pl
from jax.experimental.pallas import tpu as pltpu
from jax.sharding import PartitionSpec as P

F32 = jnp.float32
BF16 = jnp.bfloat16
LANES = 128
ROWS = 8
EDGE = 4
VMEM_BYTES = 60 * 1024 * 1024


def diffusivity_field(class_map, class_diffusivity):
    classes = jnp.arange(class_diffusivity.shape[0], dtype=jnp.int32)
    match = (class_map[None, :, :] == classes[:, None, None]).astype(jnp.float32)
    return jnp.sum(match * class_diffusivity[:, None, None], axis=0)


def diffusion_step(field, diffusivity):
    zero_row = jnp.zeros_like(field[:1])
    northern = jnp.concatenate([zero_row, field[:-1]], axis=0)
    southern = jnp.concatenate([field[1:], zero_row], axis=0)
    eastern = jnp.roll(field, -1, axis=1)
    western = jnp.roll(field, 1, axis=1)
    corners = jnp.roll(northern, -1, axis=1) + jnp.roll(northern, 1, axis=1)
    corners = corners + jnp.roll(southern, -1, axis=1) + jnp.roll(southern, 1, axis=1)
    laplace = (4.0 * (northern + southern + eastern + western) + corners - 20.0 * field) / 6.0
    return field + diffusivity * laplace


def diffuse(field, steps, diffusivity):
    return lax.fori_loop(
        jnp.int32(0), steps, lambda step_index, state: diffusion_step(state, diffusivity), field
    )


def sweep(field, keep, mix, index):
    rows, cells = field.shape[-2:]
    tiles = cells // LANES
    lane = lax.broadcasted_iota(jnp.int32, (rows, LANES), 1)
    first_lane = lane == 0
    last_lane = lane == LANES - 1

    def column(c):
        return field[index, :, c * LANES:(c + 1) * LANES]

    def from_west(value):
        return pltpu.roll(value, 1, axis=1)

    def from_east(value):
        return pltpu.roll(value, LANES - 1, axis=1)

    here = column(0)
    start_east = from_east(here)
    west_before = from_west(column(tiles - 1))
    west_here = from_west(here)
    east_here = start_east
    for c in range(tiles):
        if c + 1 < tiles:
            there = column(c + 1)
            west_there = from_west(there)
            east_there = from_east(there)
        else:
            there, west_there, east_there = None, None, start_east
        west = jnp.where(first_lane, west_before, west_here)
        east = jnp.where(last_lane, east_there, east_here)
        along = 4.0 * here + (west + east)
        across = 4.0 * along + (pltpu.roll(along, 1, axis=0) + pltpu.roll(along, rows - 1, axis=0))
        span = slice(c * LANES, (c + 1) * LANES)
        field[index, :, span] = keep[:, span] * here + mix[:, span] * across
        west_before, west_here, east_here, here = west_here, west_there, east_there, there


def product_of(pert, grad, member, level):
    total = pert[member, level, 0].astype(F32) * grad[level, 0].astype(F32)
    for v in range(1, grad.shape[1]):
        total = total + pert[member, level, v].astype(F32) * grad[level, v].astype(F32)
    return total.astype(BF16).astype(F32)


def pack_kernel(levels, steps, pert, grad, tops, bottoms, top_rows, bottom_rows, offset):
    members, block = pert.shape[:2]
    capacity = tops.shape[0]
    at = pl.program_id(0)

    @pl.when(at == 0)
    def _():
        offset[0] = 0

    for j in range(block):
        count = steps[levels[at] + j]
        for m in range(members):
            product = product_of(pert, grad, m, j)
            off = jnp.minimum(offset[0], capacity)
            for c in range(top_rows.shape[0]):
                part = product[:, c * LANES:(c + 1) * LANES]
                top_rows[c, pl.ds(off, ROWS), :] = part
                bottom_rows[c, pl.ds(capacity - off, ROWS), :] = part
            offset[0] = off + count

    @pl.when(at == pl.num_programs(0) - 1)
    def _():
        for c in range(top_rows.shape[0]):
            span = slice(c * LANES, (c + 1) * LANES)
            tops[:, span] = top_rows[c, :capacity, :].astype(BF16)
            bottoms[:, span] = bottom_rows[c, ROWS:, :].astype(BF16)


def pack_halos(pert, grad, levels, steps, block, capacity):
    members, _, variables, rows, cells = pert.shape
    blocks = grad.shape[0] // block
    out = jax.ShapeDtypeStruct((capacity, cells), BF16)
    whole = pl.BlockSpec((capacity, cells), lambda i, lv, st: (0, 0))
    return pl.pallas_call(
        pack_kernel,
        out_shape=(out, out),
        grid_spec=pltpu.PrefetchScalarGridSpec(
            num_scalar_prefetch=2,
            grid=(blocks,),
            in_specs=[
                pl.BlockSpec((members, block, variables, rows, cells), lambda i, lv, st: (0, lv[i] // block, 0, 0, 0)),
                pl.BlockSpec((block, variables, rows, cells), lambda i, lv, st: (i, 0, 0, 0)),
            ],
            out_specs=[whole, whole],
            scratch_shapes=[
                pltpu.VMEM((cells // LANES, capacity + ROWS, LANES), F32),
                pltpu.VMEM((cells // LANES, capacity + ROWS, LANES), F32),
                pltpu.SMEM((1,), jnp.int32),
            ],
        ),
        compiler_params=pltpu.CompilerParams(vmem_limit_bytes=VMEM_BYTES),
        cost_estimate=pl.CostEstimate(flops=0, transcendentals=0, bytes_accessed=grad.size * 2 * (members + 1) + 4 * capacity * cells),
        name="pack",
    )(levels, steps, pert, grad)


def deep_product_kernel(levels, pert, grad, out):
    for m in range(pert.shape[0]):
        out[m] = product_of(pert, grad, m, 0).astype(BF16)


def deep_products(pert, grad, levels, slots):
    members, _, variables, rows, cells = pert.shape
    count = levels.shape[0]
    return pl.pallas_call(
        lambda levels, slots, pert, grad, out: deep_product_kernel(levels, pert, grad, out),
        out_shape=jax.ShapeDtypeStruct((count * members, rows, cells), BF16),
        grid_spec=pltpu.PrefetchScalarGridSpec(
            num_scalar_prefetch=2,
            grid=(count,),
            in_specs=[
                pl.BlockSpec((members, 1, variables, rows, cells), lambda i, lv, sl: (0, lv[i], 0, 0, 0)),
                pl.BlockSpec((1, variables, rows, cells), lambda i, lv, sl: (sl[i], 0, 0, 0)),
            ],
            out_specs=pl.BlockSpec((members, rows, cells), lambda i, lv, sl: (i, 0, 0)),
        ),
        compiler_params=pltpu.CompilerParams(vmem_limit_bytes=VMEM_BYTES),
        cost_estimate=pl.CostEstimate(flops=0, transcendentals=0, bytes_accessed=count * members * rows * cells * 6),
        name="deep_product",
    )(levels, slots, pert, grad)


def deep_kernel(count, plane, keep, mix, out, field):
    rows = plane.shape[1]
    field[0, :rows, :] = plane[0].astype(F32)
    field[0, rows:, :] = jnp.zeros((ROWS, plane.shape[2]), F32)

    def step(i, carry):
        sweep(field, keep, mix, 0)
        return carry

    lax.fori_loop(0, count[0], step, 0)
    out[0] = field[0, :rows, :].astype(BF16)


def deep_smooth(plane, keep, mix, count):
    _, rows, cells = plane.shape
    return pl.pallas_call(
        deep_kernel,
        out_shape=jax.ShapeDtypeStruct(plane.shape, BF16),
        in_specs=[pl.BlockSpec(memory_space=pltpu.SMEM)] + [pl.BlockSpec(memory_space=pltpu.VMEM)] * 3,
        out_specs=pl.BlockSpec(memory_space=pltpu.VMEM),
        scratch_shapes=[pltpu.VMEM((1, rows + ROWS, cells), F32)],
        compiler_params=pltpu.CompilerParams(vmem_limit_bytes=VMEM_BYTES),
        cost_estimate=pl.CostEstimate(flops=150 * plane.size, transcendentals=0, bytes_accessed=plane.size * 12),
        name="deep_smooth",
    )(count, plane, keep, mix)


def smooth_kernel(levels, steps, ranks, pert, grad, below, above, keep, mix, deep, out, below_rows, above_rows, field, smooth, offset):
    members, block = pert.shape[:2]
    capacity = below.shape[0]
    top = deep.shape[0] // members
    at = pl.program_id(0)

    @pl.when(at == 0)
    def _():
        offset[0] = 0
        for c in range(below_rows.shape[0]):
            span = slice(c * LANES, (c + 1) * LANES)
            below_rows[c, :capacity, :] = below[:, span].astype(F32)
            above_rows[c, ROWS:, :] = above[:, span].astype(F32)

    row = lax.broadcasted_iota(jnp.int32, (ROWS, LANES), 0)

    def one_level(j, carry):
        level = levels[at] + j
        count = steps[level]
        rank = ranks[level]

        @pl.when(rank >= top)
        def _():
            for m in range(members):
                off = jnp.minimum(offset[0], capacity)
                field[m, :ROWS, :] = product_of(pert, grad, m, j)
                for c in range(below_rows.shape[0]):
                    field[m, ROWS:, c * LANES:(c + 1) * LANES] = jnp.where(
                        row < EDGE, below_rows[c, pl.ds(off, ROWS), :], above_rows[c, pl.ds(capacity - off, ROWS), :]
                    )
                offset[0] = off + count

            def step(i, carry):
                for m in range(members):
                    sweep(field, keep, mix, m)
                return carry

            lax.fori_loop(0, count, step, 0)
            for m in range(members):
                smooth[m] = field[m, :ROWS, :].astype(BF16)

        @pl.when(rank < top)
        def _():
            for m in range(members):
                smooth[m] = deep[rank * members + m]

        for v in range(out.shape[1]):
            total = pert[0, j, v].astype(F32) * smooth[0].astype(F32)
            for m in range(1, members):
                total = total + pert[m, j, v].astype(F32) * smooth[m].astype(F32)
            out[j, v] = total
        return carry

    lax.fori_loop(0, block, one_level, 0)


def smooth_group(pert, grad, below, above, keep, mix, deep, levels, steps, ranks, block):
    members, _, variables, rows, cells = pert.shape
    blocks = grad.shape[0] // block
    capacity = below.shape[0]

    def whole(shape):
        return pl.BlockSpec(shape, lambda i, lv, st, rk: (0,) * len(shape))

    return pl.pallas_call(
        smooth_kernel,
        out_shape=jax.ShapeDtypeStruct(grad.shape, F32),
        grid_spec=pltpu.PrefetchScalarGridSpec(
            num_scalar_prefetch=3,
            grid=(blocks,),
            in_specs=[
                pl.BlockSpec((members, block, variables, rows, cells), lambda i, lv, st, rk: (0, lv[i] // block, 0, 0, 0)),
                pl.BlockSpec((block, variables, rows, cells), lambda i, lv, st, rk: (i, 0, 0, 0)),
                whole(below.shape), whole(above.shape), whole(keep.shape), whole(mix.shape), whole(deep.shape),
            ],
            out_specs=pl.BlockSpec((block, variables, rows, cells), lambda i, lv, st, rk: (i, 0, 0, 0)),
            scratch_shapes=[
                pltpu.VMEM((cells // LANES, capacity + ROWS, LANES), F32),
                pltpu.VMEM((cells // LANES, capacity + ROWS, LANES), F32),
                pltpu.VMEM((members, 2 * ROWS, cells), F32),
                pltpu.VMEM((members, ROWS, cells), BF16),
                pltpu.SMEM((1,), jnp.int32),
            ],
        ),
        compiler_params=pltpu.CompilerParams(vmem_limit_bytes=VMEM_BYTES),
        cost_estimate=pl.CostEstimate(flops=50 * grad.size, transcendentals=0, bytes_accessed=grad.size * 2 * (members + 3)),
        name="smooth",
    )(levels, steps, ranks, pert, grad, below, above, keep, mix, deep)


def halo_program(perturbations, gradient, static_variance, level_steps, ranks, field_diffusivity, capacity):
    members, levels, variables, rows, cells = perturbations.shape
    mem_count = lax.axis_size("mem")
    tile_count = lax.axis_size("tile")
    me = lax.axis_index("mem")
    tile = lax.axis_index("tile")
    owned = gradient.shape[0]
    block = 4
    chips = mem_count // 2
    top = tile_count // members

    partner = [(i, i ^ 1) for i in range(mem_count)]

    def hop(value, d):
        return lax.ppermute(value, "mem", [(i, ((i // 2 + d) % chips) * 2 + i % 2) for i in range(mem_count)])

    def swap(value):
        return lax.ppermute(value, "mem", partner)

    steps = jnp.where(ranks < top, 0, level_steps)
    level_ids = jnp.arange(levels, dtype=jnp.int32)
    deep_levels = jnp.sum(jnp.where(ranks[None, :] == level_ids[:top, None], level_ids[None, :], 0), axis=1)

    def owner(d, other):
        return ((me // 2 - d) % chips) * 2 + (me % 2) ^ other

    def block_levels(d):
        first = jnp.stack([owner(d, 0), owner(d, 1)]) * owned
        return (first[:, None] + jnp.arange(owned // block, dtype=jnp.int32)[None, :] * block).reshape(-1)

    padded = jnp.pad(field_diffusivity, ((EDGE, EDGE), (0, 0)))
    window = lax.dynamic_slice_in_dim(padded, tile * rows, rows + 2 * EDGE)
    window = jnp.concatenate([window[EDGE:], window[:EDGE]])
    keep, mix = 1.0 - 6.0 * window, window / 6.0
    around = jnp.pad(field_diffusivity, ((0, ROWS), (0, 0)))
    deep_keep, deep_mix = 1.0 - 6.0 * around, around / 6.0

    south = [(i + 1, i) for i in range(tile_count - 1)]
    north = [(i, i + 1) for i in range(tile_count - 1)]

    groups = []
    far = [hop(gradient, d) for d in range(1, chips)]
    for d in range(chips):
        mine = gradient if d == 0 else far[d - 1]
        grad = jnp.concatenate([mine, swap(mine)])
        lv = block_levels(d)
        tops, bottoms = pack_halos(perturbations, grad, lv, steps, block, capacity)
        below = lax.ppermute(tops, "tile", south)
        above = lax.ppermute(bottoms, "tile", north)
        groups.append((grad, lv, below, above))

    all_grad = jnp.concatenate([g[0] for g in groups])
    own_order = jnp.concatenate([g[1] for g in groups])
    deep_owner = deep_levels // owned
    shift = (me // 2 - deep_owner // 2) % chips
    slots = (shift * 2 + ((me ^ deep_owner) & 1)) * owned + deep_levels % owned
    deep = deep_products(perturbations, all_grad, deep_levels, slots)
    field = lax.all_to_all(deep, "tile", split_axis=0, concat_axis=1, tiled=True)
    my_level = jnp.sum(jnp.where(level_ids[:top] == tile // members, deep_levels, 0))
    my_steps = jnp.sum(jnp.where(level_ids == my_level, level_steps, 0)).reshape(1)
    field = deep_smooth(field, deep_keep, deep_mix, my_steps)
    deep = lax.all_to_all(field, "tile", split_axis=1, concat_axis=0, tiled=True)

    total = static_variance * gradient.astype(F32)
    for d in list(range(1, chips)) + [0]:
        grad, lv, below, above = groups[d]
        part = smooth_group(perturbations, grad, below, above, keep, mix, deep, lv, steps, ranks, block)
        both = part[:owned] + swap(part[owned:])
        if d == 0:
            total = total + both
        else:
            total = total + hop(both.astype(BF16), chips - d).astype(F32)
    return total


def general_program(perturbations, gradient, static_variance, level_steps, diffusivity):
    members, levels, variables, lat_rows, lon_cells = perturbations.shape
    tile_count = lax.axis_size("tile")
    full_grad = lax.all_gather(gradient, "mem", axis=0, tiled=True)
    product = jnp.sum(
        perturbations.astype(jnp.float32) * full_grad.astype(jnp.float32)[None], axis=2
    ).astype(jnp.bfloat16)
    plane_total = members * levels
    per_dev = plane_total // tile_count
    planes = product.reshape(plane_total, lat_rows, lon_cells)
    plane_ids = jnp.arange(plane_total, dtype=jnp.int32)
    level_of = plane_ids % levels
    level_ids = jnp.arange(levels, dtype=jnp.int32)
    plane_steps = jnp.sum(
        jnp.where(level_of[:, None] == level_ids[None, :], level_steps[None, :], 0), axis=1
    )
    ranked = jnp.argsort(-plane_steps, stable=True)
    owner_index = plane_ids // per_dev
    sweep_index = plane_ids % per_dev
    position = jnp.where(sweep_index % 2 == 0, owner_index, tile_count - 1 - owner_index)
    source = ranked[sweep_index * tile_count + position]
    planes = planes[source]
    arrived = lax.all_to_all(planes, "tile", split_axis=0, concat_axis=1, tiled=True)
    device_index = lax.axis_index("tile")
    local_ids = lax.dynamic_slice_in_dim(source, device_index * per_dev, per_dev)
    local_steps = jnp.sum(
        jnp.where(local_ids[:, None] == plane_ids[None, :], plane_steps[None, :], 0), axis=1
    )

    def smooth_one(packed):
        return diffuse(packed[0].astype(jnp.float32), packed[1], diffusivity).astype(jnp.bfloat16)

    smooth = lax.map(smooth_one, (arrived, local_steps))
    returned = lax.all_to_all(smooth, "tile", split_axis=1, concat_axis=0, tiled=True)
    returned = returned[jnp.argsort(source)]
    smooth_tiles = returned.reshape(members, levels, lat_rows, lon_cells)
    partial_value = jnp.sum(
        perturbations.astype(jnp.float32) * smooth_tiles.astype(jnp.float32)[:, :, None], axis=0
    )
    reduced = lax.psum_scatter(partial_value, "mem", scatter_dimension=0, tiled=True)
    return static_variance * gradient.astype(jnp.float32) + reduced


def shards(perturbations, gradient, static_variance, level_steps, class_map, class_diffusivity):
    members, levels = perturbations.shape[:2]
    owned = gradient.shape[0]
    top = lax.axis_size("tile") // members
    capacity = (5 * members * owned + 15) // 16 * 16
    level_ids = jnp.arange(levels, dtype=jnp.int32)
    ahead = (level_steps[None, :] > level_steps[:, None]) | (
        (level_steps[None, :] == level_steps[:, None]) & (level_ids[None, :] < level_ids[:, None])
    )
    ranks = jnp.sum(ahead.astype(jnp.int32), axis=1)
    steps = jnp.where(ranks < top, 0, level_steps)
    group_rows = members * jnp.sum(steps.reshape(-1, 2 * owned), axis=1)
    fits = (jnp.max(steps) <= EDGE) & (jnp.max(group_rows) <= capacity)
    diffusivity = diffusivity_field(class_map, class_diffusivity)

    def halo(pert, grad, var, diff):
        return halo_program(pert, grad, var, level_steps, ranks, diff, capacity)

    def general(pert, grad, var, diff):
        return general_program(pert, grad, var, level_steps, diff)

    return lax.cond(fits, halo, general, perturbations, gradient, static_variance, diffusivity)


def solution(mesh):
    placed = (
        P("mem", None, None, "tile", None),
        P("mem", None, "tile", None),
        P("mem", None, "tile", None),
        P(),
        P(),
        P(),
    )
    return jax.shard_map(
        shards, mesh=mesh, in_specs=placed, out_specs=P("mem", None, "tile", None), check_vma=False
    )
```

```python
import functools
import jax
import jax.numpy as jnp
from jax import lax
from jax.experimental import pallas as pl
from jax.experimental.pallas import tpu as pltpu
from jax.sharding import PartitionSpec as P

F32 = jnp.float32
BF16 = jnp.bfloat16
I32 = jnp.int32
LANES = 128
ROWS = 8
EDGE = 4
VMEM_BYTES = 60 * 1024 * 1024
SMEM_SPEC = pl.BlockSpec(memory_space=pltpu.SMEM)
VMEM_SPEC = pl.BlockSpec(memory_space=pltpu.VMEM)
ANY_SPEC = pl.BlockSpec(memory_space=pl.ANY)


def cost(flops, size):
    return pl.CostEstimate(flops=int(flops), transcendentals=0, bytes_accessed=int(size))


def span(c):
    return slice(c * LANES, (c + 1) * LANES)


def diffuse_columns(field, keep, mix, index, first, rows, weight_first, emit):
    tiles = field.shape[1]
    lane = lax.broadcasted_iota(I32, (rows, LANES), 1)
    first_lane = lane == 0
    last_lane = lane == LANES - 1

    def load(c):
        here = field[index, c, first:first + rows, :]
        beside = field[index, c, first - 1:first - 1 + rows, :] + field[index, c, first + 1:first + 1 + rows, :]
        line = 4.0 * here + beside
        return here, line, pltpu.roll(line, 1, axis=1), pltpu.roll(line, LANES - 1, axis=1)

    here, line, to_east, to_west = load(0)
    start_west = to_west
    before = load(tiles - 1)[2]
    for c in range(tiles):
        if c + 1 < tiles:
            there = load(c + 1)
            after = there[3]
        else:
            there, after = None, start_west
        west = jnp.where(first_lane, before, to_east)
        east = jnp.where(last_lane, after, to_west)
        across = 4.0 * line + (west + east)
        place = slice(weight_first, weight_first + rows)
        emit(c, keep[c, place, :] * here + mix[c, place, :] * across)
        if there is not None:
            before = to_east
            here, line, to_east, to_west = there


def sweep(field, keep, mix, index, first, rows):
    def store(c, value):
        field[index, c, first:first + rows, :] = value

    diffuse_columns(field, keep, mix, index, first, rows, 0, store)


def diffusivity_of(classes, values, valid=None):
    total = jnp.zeros(classes.shape, F32)
    for k in range(values.shape[0]):
        total = jnp.where(classes == k, values[k], total)
    return total if valid is None else jnp.where(valid, total, 0.0)


def store_weights(keep, mix, c, place, diffusivity):
    keep[c, place, :] = 1.0 - 6.0 * diffusivity
    mix[c, place, :] = diffusivity * (1.0 / 6.0)


def product_of(pert, grad, member, level, c):
    total = None
    for v in range(grad.shape[1]):
        term = pert[member, level, v, :, span(c)].astype(F32) * grad[level, v, :, span(c)].astype(F32)
        total = term if total is None else total + term
    return total.astype(BF16)


def pack_kernel(first, steps, pert, near, far, tops, bottoms, top_rows, bottom_rows, offset):
    members, block = pert.shape[:2]
    capacity = tops.shape[0]
    at = pl.program_id(0)
    half = pl.num_programs(0) // 2

    @pl.when(at == 0)
    def _():
        offset[0] = 0

    def pack(grad):
        for j in range(block):
            count = steps[first[at] + j]
            for m in range(members):
                off = jnp.minimum(offset[0], capacity)
                for c in range(top_rows.shape[0]):
                    part = product_of(pert, grad, m, j, c).astype(F32)
                    top_rows[c, pl.ds(off, ROWS), :] = part
                    bottom_rows[c, pl.ds(capacity - off, ROWS), :] = part
                offset[0] = off + count

    @pl.when(at < half)
    def _():
        pack(near)

    @pl.when(at >= half)
    def _():
        pack(far)

    @pl.when(at == 2 * half - 1)
    def _():
        for c in range(top_rows.shape[0]):
            tops[:, span(c)] = top_rows[c, :capacity, :].astype(BF16)
            bottoms[:, span(c)] = bottom_rows[c, ROWS:, :].astype(BF16)


def pack_halos(pert, near, far, owners, steps, block, capacity):
    members, _, variables, rows, cells = pert.shape
    owned = near.shape[0]
    blocks = owned // block
    first = (owners[:, None] * owned + block * jnp.arange(blocks, dtype=I32)[None, :]).reshape(-1)
    out = jax.ShapeDtypeStruct((capacity, cells), BF16)
    whole = pl.BlockSpec((capacity, cells), lambda i, lv, st: (0, 0))
    grad_block = (block, variables, rows, cells)
    return pl.pallas_call(
        pack_kernel,
        out_shape=(out, out),
        grid_spec=pltpu.PrefetchScalarGridSpec(
            num_scalar_prefetch=2,
            grid=(2 * blocks,),
            in_specs=[
                pl.BlockSpec((members,) + grad_block, lambda i, lv, st: (0, lv[i] // block, 0, 0, 0)),
                pl.BlockSpec(grad_block, lambda i, lv, st: (jnp.minimum(i, blocks - 1), 0, 0, 0)),
                pl.BlockSpec(grad_block, lambda i, lv, st: (jnp.maximum(i - blocks, 0), 0, 0, 0)),
            ],
            out_specs=[whole, whole],
            scratch_shapes=[
                pltpu.VMEM((cells // LANES, capacity + ROWS, LANES), F32),
                pltpu.VMEM((cells // LANES, capacity + ROWS, LANES), F32),
                pltpu.SMEM((1,), I32),
            ],
        ),
        compiler_params=pltpu.CompilerParams(vmem_limit_bytes=VMEM_BYTES),
        cost_estimate=cost(8 * near.size, 2 * near.size * 2 * (members + 1)),
    )(first, steps, pert, near, far)


def deep_product_kernel(levels, me, pert, *rest):
    grads, (out, pert_rows, grad_rows, pert_sem, grad_sem) = rest[:-5], rest[-5:]
    count, members = pert_rows.shape[:2]
    owned = grads[0].shape[0]
    planes = count * members
    chips = len(grads) // 2

    def pert_copy(k):
        return pltpu.make_async_copy(pert.at[:, levels[k]], pert_rows.at[k], pert_sem.at[k])

    def grad_copy(g, k):
        return pltpu.make_async_copy(grads[g].at[levels[k] % owned], grad_rows.at[k], grad_sem.at[k])

    def begin(k, carry):
        owner = levels[k] // owned
        shift = lax.rem(me[0] // 2 - owner // 2 + chips, chips)
        place = 2 * shift + lax.rem(me[0] + owner, 2)
        pert_copy(k).start()
        for g in range(len(grads)):
            @pl.when(place == g)
            def _():
                grad_copy(g, k).start()
        return carry

    lax.fori_loop(0, count, begin, 0)
    per_device = me[1]

    def form(k, carry):
        pert_copy(k).wait()
        grad_copy(0, k).wait()
        for m in range(members):
            q = k * members + m
            place = deep_place(q, planes, per_device)
            for c in range(pert.shape[-1] // LANES):
                total = None
                for v in range(pert.shape[2]):
                    term = pert_rows[k, m, v, :, span(c)].astype(F32) * grad_rows[k, v, :, span(c)].astype(F32)
                    total = term if total is None else total + term
                out[place, :, span(c)] = total.astype(BF16)
        return carry

    lax.fori_loop(0, count, form, 0)


def deep_products(pert, grads, levels, me, per_device):
    members, _, variables, rows, cells = pert.shape
    count = levels.shape[0]
    info = jnp.stack([me, jnp.int32(per_device)])
    return pl.pallas_call(
        deep_product_kernel,
        out_shape=jax.ShapeDtypeStruct((count * members, rows, cells), BF16),
        in_specs=[SMEM_SPEC, SMEM_SPEC] + [ANY_SPEC] * (1 + len(grads)),
        out_specs=VMEM_SPEC,
        scratch_shapes=[
            pltpu.VMEM((count, members, variables, rows, cells), BF16),
            pltpu.VMEM((count, variables, rows, cells), BF16),
            pltpu.SemaphoreType.DMA((count,)),
            pltpu.SemaphoreType.DMA((count,)),
        ],
        compiler_params=pltpu.CompilerParams(vmem_limit_bytes=VMEM_BYTES),
        cost_estimate=cost(count * members * rows * cells * 4, count * members * rows * cells * 8),
        name="deep_product",
    )(levels, info, pert, *grads)


def deep_kernel(counts, values, planes, class_map, out, field, keep, mix):
    at = pl.program_id(0)
    parts, _, rows, _ = planes.shape
    height = parts * rows
    tiles = field.shape[1]

    @pl.when(at == 0)
    def _():
        for c in range(tiles):
            field[0, c, :ROWS, :] = jnp.zeros((ROWS, LANES), F32)
            field[0, c, ROWS + height:, :] = jnp.zeros((ROWS, LANES), F32)
            store_weights(keep, mix, c, slice(0, height), diffusivity_of(class_map[:, span(c)], values))

    for p in range(parts):
        for c in range(tiles):
            field[0, c, ROWS + p * rows:ROWS + (p + 1) * rows, :] = planes[p, 0, :, span(c)].astype(F32)

    def step(i, carry):
        sweep(field, keep, mix, 0, ROWS, height)
        return carry

    lax.fori_loop(0, counts[at], step, 0)
    for p in range(parts):
        for c in range(tiles):
            out[p, 0, :, span(c)] = field[0, c, ROWS + p * rows:ROWS + (p + 1) * rows, :].astype(BF16)


def deep_smooth(planes, class_map, values, counts):
    parts, per_device, rows, cells = planes.shape
    tiles = cells // LANES
    plane = pl.BlockSpec((parts, 1, rows, cells), lambda i: (0, i, 0, 0))
    return pl.pallas_call(
        deep_kernel,
        out_shape=jax.ShapeDtypeStruct(planes.shape, BF16),
        grid=(per_device,),
        in_specs=[SMEM_SPEC, SMEM_SPEC, plane, VMEM_SPEC],
        out_specs=plane,
        scratch_shapes=[
            pltpu.VMEM((1, tiles, parts * rows + 2 * ROWS, LANES), F32),
            pltpu.VMEM((tiles, parts * rows, LANES), F32),
            pltpu.VMEM((tiles, parts * rows, LANES), F32),
        ],
        compiler_params=pltpu.CompilerParams(vmem_limit_bytes=VMEM_BYTES),
        cost_estimate=cost(150 * planes.size, planes.size * 4 + parts * rows * cells * 4),
        name="deep_smooth",
    )(counts, values, planes, class_map)


def deep_place(q, planes, per_device):
    devices = planes // per_device
    return lax.rem(q, devices) * per_device + q // devices


def smooth_kernel(with_deep, with_part, with_variance, info, steps, ranks, values, pert, grad, below, above, before, here, after, *rest):
    extra, (out, below_rows, above_rows, field, keep, mix, offset) = rest[:-7], rest[-7:]
    deep = extra[0] if with_deep else None
    extra = extra[1:] if with_deep else extra
    members, block = pert.shape[:2]
    capacity = below.shape[0]
    tiles = field.shape[1]
    owned = pl.num_programs(0) * block
    planes = deep.shape[0] if with_deep else 0
    at = pl.program_id(0)
    row = lax.broadcasted_iota(I32, (ROWS, LANES), 0)

    @pl.when(at == 0)
    def _():
        start = jnp.int32(0)
        for j in range(owned):
            start = start + steps[jnp.maximum(info[1], 0) + j]
        offset[0] = jnp.where(info[1] >= 0, members * start, 0)
        inside_before = jnp.broadcast_to(info[2] > 0, (ROWS, LANES))
        inside_after = jnp.broadcast_to(info[2] < info[3] - 1, (ROWS, LANES))
        for c in range(tiles):
            below_rows[c, :capacity, :] = below[:, span(c)].astype(F32)
            below_rows[c, capacity:, :] = jnp.zeros((ROWS, LANES), F32)
            above_rows[c, ROWS:, :] = above[:, span(c)].astype(F32)
            above_rows[c, :ROWS, :] = jnp.zeros((ROWS, LANES), F32)
            upper = diffusivity_of(before[:, span(c)], values, inside_before)
            lower = diffusivity_of(after[:, span(c)], values, inside_after)
            store_weights(keep, mix, c, slice(0, EDGE), upper[ROWS - EDGE:])
            store_weights(keep, mix, c, slice(EDGE, EDGE + ROWS), diffusivity_of(here[:, span(c)], values))
            store_weights(keep, mix, c, slice(EDGE + ROWS, 2 * EDGE + ROWS), lower[:EDGE])

    def one_level(j, carry):
        level = info[0] + at * block + j
        count = steps[level]
        rank = ranks[level]

        @pl.when(rank >= info[4])
        def _():
            for m in range(members):
                off = jnp.minimum(offset[0], capacity)
                for c in range(tiles):
                    field[m, c, :ROWS, :] = above_rows[c, pl.ds(capacity - off, ROWS), :]
                    field[m, c, ROWS:2 * ROWS, :] = product_of(pert, grad, m, j, c).astype(F32)
                    field[m, c, 2 * ROWS:, :] = below_rows[c, pl.ds(off, ROWS), :]
                offset[0] = off + count

            def step(i, carry):
                for m in range(members):
                    sweep(field, keep, mix, m, ROWS - EDGE, ROWS + 2 * EDGE)
                return carry

            lax.fori_loop(1, count, step, 0)

            for m in range(members):
                def store(c, value):
                    field[m, c, ROWS:2 * ROWS, :] = value

                diffuse_columns(field, keep, mix, m, ROWS, ROWS, EDGE, store)

        if deep is None:
            @pl.when(rank < info[4])
            def _():
                for m in range(members):
                    for c in range(tiles):
                        field[m, c, ROWS:2 * ROWS, :] = jnp.zeros((ROWS, LANES), F32)
        else:
            @pl.when(rank < info[4])
            def _():
                for m in range(members):
                    place = deep_place(rank * members + m, planes, info[5])
                    for c in range(tiles):
                        field[m, c, ROWS:2 * ROWS, :] = deep[place, :, span(c)].astype(F32)

        for c in range(tiles):
            smooth = [field[m, c, ROWS:2 * ROWS, :].astype(BF16).astype(F32) for m in range(members)]
            for v in range(out.shape[1]):
                total = None
                for m in range(members):
                    term = pert[m, j, v, :, span(c)].astype(F32) * smooth[m]
                    total = term if total is None else total + term
                if with_part:
                    total = total + extra[0][j, v, :, span(c)].astype(F32)
                if with_variance:
                    total = total + extra[0][j, v, :, span(c)] * grad[j, v, :, span(c)].astype(F32)
                out[j, v, :, span(c)] = total.astype(out.dtype)
        return carry

    lax.fori_loop(0, block, one_level, 0)


def smooth_owner(pert, grad, halos, class_map, deep, part, variance, info, steps, ranks, values, block, dtype):
    members, _, variables, rows, cells = pert.shape
    tiles = cells // LANES
    capacity = halos[0].shape[0]
    extra = [x for x in (part, variance) if x is not None]
    whole_deep = [] if deep is None else [deep]
    kernel = functools.partial(smooth_kernel, deep is not None, part is not None, variance is not None)
    row_tiles = class_map.shape[0] // rows

    def whole(shape):
        return pl.BlockSpec(shape, lambda i, *refs: (0,) * len(shape))

    def rows_at(shift):
        return pl.BlockSpec((rows, cells), lambda i, info, *refs: (jnp.clip(info[2] + shift, 0, row_tiles - 1), 0))

    grad_block = pl.BlockSpec((block, variables, rows, cells), lambda i, *refs: (i, 0, 0, 0))
    return pl.pallas_call(
        kernel,
        out_shape=jax.ShapeDtypeStruct(grad.shape, dtype),
        grid_spec=pltpu.PrefetchScalarGridSpec(
            num_scalar_prefetch=4,
            grid=(grad.shape[0] // block,),
            in_specs=[
                pl.BlockSpec((members, block, variables, rows, cells), lambda i, info, *refs: (0, info[0] // block + i, 0, 0, 0)),
                grad_block,
                whole(halos[0].shape), whole(halos[1].shape), rows_at(-1), rows_at(0), rows_at(1),
            ] + [whole(x.shape) for x in whole_deep] + [grad_block] * len(extra),
            out_specs=grad_block,
            scratch_shapes=[
                pltpu.VMEM((tiles, capacity + ROWS, LANES), F32),
                pltpu.VMEM((tiles, capacity + ROWS, LANES), F32),
                pltpu.VMEM((members, tiles, 3 * ROWS, LANES), F32),
                pltpu.VMEM((tiles, 2 * EDGE + ROWS, LANES), F32),
                pltpu.VMEM((tiles, 2 * EDGE + ROWS, LANES), F32),
                pltpu.SMEM((1,), I32),
            ],
        ),
        compiler_params=pltpu.CompilerParams(vmem_limit_bytes=VMEM_BYTES),
        cost_estimate=cost(100 * grad.size, grad.size * 2 * (members + 3)),
    )(info, steps, ranks, values, pert, grad, halos[0], halos[1], class_map, class_map, class_map, *whole_deep, *extra)


def final_kernel(info, ranks, pert, near, part, deep, *rest):
    arrived, out = rest[:-1], rest[-1]
    members = pert.shape[0]
    at = pl.program_id(0)
    rank = ranks[info[0] + at]
    planes = deep.shape[0]

    def terms(v, c):
        total = near[0, v, :, span(c)] + part[0, v, :, span(c)].astype(F32)
        for value in arrived:
            total = total + value[0, v, :, span(c)].astype(F32)
        return total

    @pl.when(rank >= info[4])
    def _():
        for v in range(out.shape[1]):
            for c in range(out.shape[3] // LANES):
                out[0, v, :, span(c)] = terms(v, c)

    @pl.when(rank < info[4])
    def _():
        for v in range(out.shape[1]):
            for c in range(out.shape[3] // LANES):
                total = terms(v, c)
                for m in range(members):
                    smooth = deep[deep_place(rank * members + m, planes, info[5]), :, span(c)].astype(F32)
                    total = total + pert[m, 0, v, :, span(c)].astype(F32) * smooth
                out[0, v, :, span(c)] = total


def final_sum(pert, near, part, deep, arrived, info, ranks):
    members, _, variables, rows, cells = pert.shape
    block = pl.BlockSpec((1, variables, rows, cells), lambda i, *refs: (i, 0, 0, 0))

    def deep_level(i, info, ranks):
        return (0, info[0] + jnp.where(ranks[info[0] + i] < info[4], i, 0), 0, 0, 0)

    return pl.pallas_call(
        final_kernel,
        out_shape=jax.ShapeDtypeStruct(near.shape, F32),
        grid_spec=pltpu.PrefetchScalarGridSpec(
            num_scalar_prefetch=2,
            grid=(near.shape[0],),
            in_specs=[
                pl.BlockSpec((members, 1, variables, rows, cells), deep_level),
                block, block, pl.BlockSpec(deep.shape, lambda i, *refs: (0, 0, 0)),
            ] + [block] * len(arrived),
            out_specs=block,
        ),
        compiler_params=pltpu.CompilerParams(vmem_limit_bytes=VMEM_BYTES),
        cost_estimate=cost(4 * near.size, near.size * 12),
        name="final_sum",
    )(info, ranks, pert, near, part, deep, *arrived)


def program(pert, gradient, variance, class_map, values, level_steps, ranks, top, capacity):
    members, levels, _, rows, cells = pert.shape
    mem_count = lax.axis_size("mem")
    tile_count = lax.axis_size("tile")
    me = lax.axis_index("mem")
    tile = lax.axis_index("tile")
    owned = gradient.shape[0]
    block = 4
    chips = mem_count // 2
    per_device = top * members // tile_count
    level_ids = jnp.arange(levels, dtype=I32)

    def hop(value, d):
        return lax.ppermute(value, "mem", [(i, ((i // 2 + d) % chips) * 2 + i % 2) for i in range(mem_count)])

    def swap(value):
        return lax.ppermute(value, "mem", [(i, i ^ 1) for i in range(mem_count)])

    south = [(i + 1, i) for i in range(tile_count - 1)]
    north = [(i, i + 1) for i in range(tile_count - 1)]

    steps = jnp.where(ranks < top, 0, level_steps)
    here = ranks[None, :] == level_ids[:top, None]
    deep_levels = jnp.sum(jnp.where(here, level_ids[None, :], 0), axis=1)
    deep_steps = jnp.sum(jnp.where(here, level_steps[None, :], 0), axis=1)
    my_ranks = (jnp.arange(per_device, dtype=I32) * tile_count + tile) // members
    my_steps = jnp.sum(jnp.where(my_ranks[:, None] == level_ids[None, :top], deep_steps[None, :], 0), axis=1)

    def owner(d, other):
        return ((me // 2 - d) % chips) * 2 + ((me % 2) ^ other)

    grads, halos = [], []
    far = []
    for d in range(1, chips):
        far.append(hop(gradient, d))
    for d in range(chips):
        near = gradient if d == 0 else far[d - 1]
        other = swap(near)
        grads += [near, other]
        if top < levels:
            owners = jnp.stack([owner(d, 0), owner(d, 1)])
            tops, bottoms = pack_halos(pert, near, other, owners, steps, block, capacity)
            below = lax.ppermute(tops, "tile", south)
            above = lax.ppermute(bottoms, "tile", north)
            halos.append((below, above))
        else:
            halos.append((jnp.zeros((16, cells), BF16),) * 2)

    deep = deep_products(pert, grads, deep_levels, me, per_device)
    deep = deep.reshape(tile_count, per_device, rows, cells)
    field = lax.all_to_all(deep, "tile", split_axis=0, concat_axis=0, tiled=True)
    field = deep_smooth(field, class_map, values, my_steps)
    deep = lax.all_to_all(field, "tile", split_axis=0, concat_axis=0, tiled=True).reshape(-1, rows, cells)

    def info_of(d, other):
        first = owner(d, other) * owned
        ahead = owner(d, 0) * owned if other else jnp.int32(-1)
        return jnp.stack([first, ahead, tile, jnp.int32(tile_count), jnp.int32(top), jnp.int32(per_device)])

    def smooth(d, other, whole, part, var, dtype):
        return smooth_owner(
            pert, grads[2 * d + other], halos[d], class_map, whole, part, var, info_of(d, other), steps, ranks, values, block, dtype
        )

    near_sum = smooth(0, 0, None, None, variance, F32)
    arrived = []
    for d in range(1, chips):
        part = smooth(d, 1, deep, None, None, BF16)
        part = swap(part)
        both = smooth(d, 0, deep, part, None, BF16)
        arrived.append(hop(both, chips - d))
    part = smooth(0, 1, deep, None, None, BF16)
    part = swap(part)
    return final_sum(pert, near_sum, part, deep, arrived, info_of(0, 0), ranks)


def shards(perturbations, gradient, static_variance, level_steps, class_map, class_diffusivity):
    members, levels = perturbations.shape[:2]
    owned = gradient.shape[0]
    top = lax.axis_size("tile") // members
    capacity = (5 * members * owned + 15) // 16 * 16
    level_ids = jnp.arange(levels, dtype=I32)
    ahead = (level_steps[None, :] > level_steps[:, None]) | (
        (level_steps[None, :] == level_steps[:, None]) & (level_ids[None, :] < level_ids[:, None])
    )
    ranks = jnp.sum(ahead.astype(I32), axis=1)
    steps = jnp.where(ranks < top, 0, level_steps)
    group_rows = members * jnp.sum(steps.reshape(-1, 2 * owned), axis=1)
    fits = (jnp.max(steps) <= EDGE) & (jnp.max(group_rows) <= capacity)
    operands = (perturbations, gradient, static_variance, class_map, class_diffusivity, level_steps, ranks)

    result = program(*operands, top, capacity)

    def general(result, *operands):
        return program(*operands, levels, 16)

    return lax.cond(fits, lambda result, *operands: result, general, result, *operands)


def solution(mesh):
    placed = (
        P("mem", None, None, "tile", None),
        P("mem", None, "tile", None),
        P("mem", None, "tile", None),
        P(),
        P(),
        P(),
    )
    return jax.shard_map(
        shards, mesh=mesh, in_specs=placed, out_specs=P("mem", None, "tile", None), check_vma=False
    )
```

```python
import functools
import jax
import jax.numpy as jnp
from jax import lax
from jax.experimental import pallas as pl
from jax.experimental.pallas import tpu as pltpu
from jax.sharding import PartitionSpec as P

F32 = jnp.float32
BF16 = jnp.bfloat16
I32 = jnp.int32
LANES = 128
ROWS = 8
EDGE = 4
PARTS = 2
VMEM_BYTES = 67043328
SMEM_SPEC = pl.BlockSpec(memory_space=pltpu.SMEM)
VMEM_SPEC = pl.BlockSpec(memory_space=pltpu.VMEM)
ANY_SPEC = pl.BlockSpec(memory_space=pl.ANY)


def cost(flops, size):
    return pl.CostEstimate(flops=int(flops), transcendentals=0, bytes_accessed=int(size))


def span(c):
    return slice(c * LANES, (c + 1) * LANES)


def diffuse_columns(field, keep, mix, index, first, rows, weight_first):
    tiles = field.shape[1]
    lane = lax.broadcasted_iota(I32, (rows, LANES), 1)
    first_lane = lane == 0
    last_lane = lane == LANES - 1

    def load(c):
        here = field[index, c, first:first + rows, :]
        beside = field[index, c, first - 1:first - 1 + rows, :] + field[index, c, first + 1:first + 1 + rows, :]
        line = 4.0 * here + beside
        return here, line, pltpu.roll(line, 1, axis=1), pltpu.roll(line, LANES - 1, axis=1)

    here, line, to_east, to_west = load(0)
    start_west = to_west
    before = load(tiles - 1)[2]
    for c in range(tiles):
        if c + 1 < tiles:
            there = load(c + 1)
            after = there[3]
        else:
            there, after = None, start_west
        west = jnp.where(first_lane, before, to_east)
        east = jnp.where(last_lane, after, to_west)
        across = 4.0 * line + (west + east)
        place = slice(weight_first, weight_first + rows)
        yield keep[c, place, :] * here + mix[c, place, :] * across
        if there is not None:
            before = to_east
            here, line, to_east, to_west = there


def sweep(field, keep, mix, index, first, rows):
    for c, value in enumerate(diffuse_columns(field, keep, mix, index, first, rows, 0)):
        field[index, c, first:first + rows, :] = value


def diffusivity_of(classes, values, valid=None):
    total = jnp.zeros(classes.shape, F32)
    for k in range(values.shape[0]):
        total = jnp.where(classes == k, values[k], total)
    return total if valid is None else jnp.where(valid, total, 0.0)


def store_weights(keep, mix, c, place, diffusivity):
    keep[c, place, :] = 1.0 - 6.0 * diffusivity
    mix[c, place, :] = diffusivity * (1.0 / 6.0)


class Plan:
    ME, TILE, FITS = 0, 1, 2

    def __init__(self, levels, top, per_device):
        self.steps = 8
        self.ranks = self.steps + levels
        self.deep = self.ranks + levels
        self.mine = self.deep + top + 1
        self.size = self.mine + per_device


BINS = 16


def plan_kernel(places, top, per_device, owned, members, capacity, position, level_steps, values, before, here, after, plan, keep, mix, bins, deep_steps):
    levels = level_steps.shape[0]
    me, tile, tile_count = position[0], position[1], position[2]
    plan[places.ME] = me
    plan[places.TILE] = tile
    for i in range(3, 8):
        plan[i] = 0

    def bin_of(level):
        return jnp.clip(level_steps[level], 0, BINS - 1)

    for i in range(BINS):
        bins[i] = 0

    def count(level, carry):
        bins[bin_of(level)] += 1
        return carry

    lax.fori_loop(0, levels, count, 0)
    total = jnp.int32(0)
    for i in reversed(range(BINS)):
        here_count = bins[i]
        bins[i] = total
        total = total + here_count

    def assign(level, carry):
        rows, most_rows, most_steps = carry
        b = bin_of(level)
        rank = bins[b]
        bins[b] = rank + 1
        whole = rank < top
        steps = jnp.where(whole, 0, level_steps[level])
        plan[places.ranks + level] = rank
        plan[places.steps + level] = steps
        slot = jnp.minimum(rank, top)
        plan[places.deep + slot] = level
        deep_steps[slot] = level_steps[level]
        rows = jnp.where(lax.rem(level, 2 * owned) == 0, 0, rows) + members * steps
        return rows, jnp.maximum(most_rows, rows), jnp.maximum(most_steps, steps)

    _, most_rows, most_steps = lax.fori_loop(0, levels, assign, (jnp.int32(0), jnp.int32(0), jnp.int32(0)))
    plan[places.FITS] = ((most_rows <= capacity) & (most_steps <= EDGE)).astype(I32)
    plan[places.deep + top] = 0
    for j in range(per_device):
        plan[places.mine + j] = deep_steps[(j * tile_count + tile) // members]

    inside_before = jnp.broadcast_to(tile > 0, (ROWS, LANES))
    inside_after = jnp.broadcast_to(tile < tile_count - 1, (ROWS, LANES))
    for c in range(keep.shape[0]):
        upper = diffusivity_of(before[:, span(c)], values, inside_before)
        lower = diffusivity_of(after[:, span(c)], values, inside_after)
        store_weights(keep, mix, c, slice(0, EDGE), upper[ROWS - EDGE:])
        store_weights(keep, mix, c, slice(EDGE, EDGE + ROWS), diffusivity_of(here[:, span(c)], values))
        store_weights(keep, mix, c, slice(EDGE + ROWS, 2 * EDGE + ROWS), lower[:EDGE])


def make_plan(places, top, per_device, owned, members, capacity, position, level_steps, values, class_map, rows):
    cells = class_map.shape[1]
    tiles = cells // LANES
    row_tiles = class_map.shape[0] // rows
    weights = jax.ShapeDtypeStruct((tiles, 2 * EDGE + rows, LANES), F32)
    weight_spec = pl.BlockSpec(weights.shape, lambda i, *refs: (0, 0, 0))

    def rows_at(shift):
        return pl.BlockSpec((rows, cells), lambda i, position, *refs: (jnp.clip(position[1] + shift, 0, row_tiles - 1), 0))

    return pl.pallas_call(
        functools.partial(plan_kernel, places, top, per_device, owned, members, capacity),
        out_shape=(jax.ShapeDtypeStruct((places.size,), I32), weights, weights),
        grid_spec=pltpu.PrefetchScalarGridSpec(
            num_scalar_prefetch=3,
            grid=(1,),
            in_specs=[rows_at(-1), rows_at(0), rows_at(1)],
            out_specs=[SMEM_SPEC, weight_spec, weight_spec],
            scratch_shapes=[pltpu.SMEM((BINS,), I32), pltpu.SMEM((top + 1,), I32)],
        ),
        compiler_params=pltpu.CompilerParams(vmem_limit_bytes=VMEM_BYTES),
        cost_estimate=cost(0, 4 * weights.size * 2),
        name="plan",
    )(position, level_steps, values, class_map, class_map, class_map)


def owner_of(me, chips, d, other):
    return lax.rem(me // 2 - d + chips, chips) * 2 + lax.rem(me + other, 2)


def product_of(pert, grad, member, level, c):
    total = None
    for v in range(grad.shape[1]):
        term = pert[member, level, v, :, span(c)].astype(F32) * grad[level, v, :, span(c)].astype(F32)
        total = term if total is None else total + term
    return total.astype(BF16)


def pack_kernel(places, chips, d, plan, pert, near, far, tops, bottoms, top_rows, bottom_rows, offset):
    members, block = pert.shape[:2]
    capacity = tops.shape[0]
    at = pl.program_id(0)
    half = pl.num_programs(0) // 2
    owned = half * block

    @pl.when(at == 0)
    def _():
        offset[0] = 0

    def pack(grad, other, i):
        first = owner_of(plan[places.ME], chips, d, other) * owned + i * block
        for j in range(block):
            count = plan[places.steps + first + j]
            for m in range(members):
                off = jnp.minimum(offset[0], capacity)
                for c in range(top_rows.shape[0]):
                    part = product_of(pert, grad, m, j, c).astype(F32)
                    top_rows[c, pl.ds(off, ROWS), :] = part
                    bottom_rows[c, pl.ds(capacity - off, ROWS), :] = part
                offset[0] = off + count

    @pl.when(at < half)
    def _():
        pack(near, 0, at)

    @pl.when(at >= half)
    def _():
        pack(far, 1, at - half)

    @pl.when(at == 2 * half - 1)
    def _():
        for c in range(top_rows.shape[0]):
            tops[:, span(c)] = top_rows[c, :capacity, :].astype(BF16)
            bottoms[:, span(c)] = bottom_rows[c, ROWS:, :].astype(BF16)


def pack_halos(places, chips, d, plan, pert, near, far, block, capacity):
    members, _, variables, rows, cells = pert.shape
    blocks = near.shape[0] // block
    out = jax.ShapeDtypeStruct((capacity, cells), BF16)
    whole = pl.BlockSpec((capacity, cells), lambda i, plan: (0, 0))
    grad_block = (block, variables, rows, cells)

    def pert_place(i, plan):
        other = i // blocks
        return (0, owner_of(plan[places.ME], chips, d, other) * blocks + lax.rem(i, blocks), 0, 0, 0)

    return pl.pallas_call(
        functools.partial(pack_kernel, places, chips, d),
        out_shape=(out, out),
        grid_spec=pltpu.PrefetchScalarGridSpec(
            num_scalar_prefetch=1,
            grid=(2 * blocks,),
            in_specs=[
                pl.BlockSpec((members,) + grad_block, pert_place),
                pl.BlockSpec(grad_block, lambda i, plan: (jnp.minimum(i, blocks - 1), 0, 0, 0)),
                pl.BlockSpec(grad_block, lambda i, plan: (jnp.maximum(i - blocks, 0), 0, 0, 0)),
            ],
            out_specs=[whole, whole],
            scratch_shapes=[
                pltpu.VMEM((cells // LANES, capacity + ROWS, LANES), F32),
                pltpu.VMEM((cells // LANES, capacity + ROWS, LANES), F32),
                pltpu.SMEM((1,), I32),
            ],
        ),
        compiler_params=pltpu.CompilerParams(vmem_limit_bytes=VMEM_BYTES),
        cost_estimate=cost(8 * near.size, 2 * near.size * 2 * (members + 1)),
    )(plan, pert, near, far)


def deep_product_kernel(places, chips, per_device, group, plan, *refs):
    perts, grads, out = refs[:group], refs[group:-1], refs[-1]
    members = perts[0].shape[0]
    count = len(grads) // group

    for u in range(group):
        k = pl.program_id(0) * group + u
        pert = perts[u]
        place = grad_place(places, chips, count, plan, k)[0]

        def form(grad):
            for m in range(members):
                spot = deep_place(k * members + m, out.shape[0], per_device)
                for c in range(pert.shape[-1] // LANES):
                    out[spot, :, span(c)] = product_of(pert, grad, m, 0, c)

        for g in range(count):
            pl.when(place == g)(functools.partial(form, grads[u * count + g]))


def grad_place(places, chips, count, plan, k):
    levels = places.ranks - places.steps
    owned = levels // count
    level = plan[places.deep + k]
    owner = level // owned
    shift = lax.rem(plan[places.ME] // 2 - owner // 2 + chips, chips)
    return 2 * shift + lax.rem(plan[places.ME] + owner, 2), lax.rem(level, owned)


def deep_products(places, chips, plan, pert, grads, top, per_device):
    members, _, variables, rows, cells = pert.shape
    group = 4 if top % 4 == 0 else 1

    def pert_spec(u):
        return pl.BlockSpec((members, 1, variables, rows, cells), lambda i, plan: (0, plan[places.deep + i * group + u], 0, 0, 0))

    def grad_spec(u, g):
        def where(i, plan):
            place, level = grad_place(places, chips, len(grads), plan, i * group + u)
            return (jnp.where(place == g, level, 0), 0, 0, 0)

        return pl.BlockSpec((1, variables, rows, cells), where)

    return pl.pallas_call(
        functools.partial(deep_product_kernel, places, chips, per_device, group),
        out_shape=jax.ShapeDtypeStruct((top * members, rows, cells), BF16),
        grid_spec=pltpu.PrefetchScalarGridSpec(
            num_scalar_prefetch=1,
            grid=(top // group,),
            in_specs=[pert_spec(u) for u in range(group)] + [grad_spec(u, g) for u in range(group) for g in range(len(grads))],
            out_specs=pl.BlockSpec((top * members, rows, cells), lambda i, plan: (0, 0, 0)),
        ),
        compiler_params=pltpu.CompilerParams(vmem_limit_bytes=VMEM_BYTES),
        cost_estimate=cost(top * members * rows * cells * 4, top * members * rows * cells * 8),
        name="deep_product",
    )(plan, *([pert] * group), *(list(grads) * group))


def deep_kernel(mine, plan, values, planes, class_map, out, field, keep, mix):
    at = pl.program_id(0)
    parts, _, rows, _ = planes.shape
    height = parts * rows
    tiles = field.shape[1]

    @pl.when(at == 0)
    def _():
        for c in range(tiles):
            field[0, c, :ROWS, :] = jnp.zeros((ROWS, LANES), F32)
            field[0, c, ROWS + height:, :] = jnp.zeros((ROWS, LANES), F32)
            store_weights(keep, mix, c, slice(0, height), diffusivity_of(class_map[:, span(c)], values))

    for p in range(parts):
        for c in range(tiles):
            field[0, c, ROWS + p * rows:ROWS + (p + 1) * rows, :] = planes[p, 0, :, span(c)].astype(F32)

    def step(i, carry):
        sweep(field, keep, mix, 0, ROWS, height)
        return carry

    lax.fori_loop(0, plan[mine + at], step, 0)
    for p in range(parts):
        for c in range(tiles):
            out[p, 0, :, span(c)] = field[0, c, ROWS + p * rows:ROWS + (p + 1) * rows, :].astype(BF16)


def deep_smooth(places, plan, planes, class_map, values):
    parts, per_device, rows, cells = planes.shape
    tiles = cells // LANES
    plane = pl.BlockSpec((parts, 1, rows, cells), lambda i: (0, i, 0, 0))
    return pl.pallas_call(
        functools.partial(deep_kernel, places.mine),
        out_shape=jax.ShapeDtypeStruct(planes.shape, BF16),
        grid=(per_device,),
        in_specs=[SMEM_SPEC, SMEM_SPEC, plane, VMEM_SPEC],
        out_specs=plane,
        scratch_shapes=[
            pltpu.VMEM((1, tiles, parts * rows + 2 * ROWS, LANES), F32),
            pltpu.VMEM((tiles, parts * rows, LANES), F32),
            pltpu.VMEM((tiles, parts * rows, LANES), F32),
        ],
        compiler_params=pltpu.CompilerParams(vmem_limit_bytes=VMEM_BYTES),
        cost_estimate=cost(150 * planes.size, planes.size * 4 + parts * rows * cells * 4),
        name="deep_smooth",
    )(plan, values, planes, class_map)


def deep_place(q, planes, per_device):
    devices = planes // per_device
    return lax.rem(q, devices) * per_device + q // devices


def smooth_kernel(places, chips, d, other, low, owned, top, per_device, with_deep, with_part, with_variance, plan, pert, grad, below, above, keep, mix, *rest):
    extra, (out, below_rows, above_rows, field, offset) = rest[:-5], rest[-5:]
    if with_deep:
        deep, extra = extra[0], extra[1:]
    members, block = pert.shape[:2]
    capacity = below.shape[0]
    tiles = field.shape[1]
    at = pl.program_id(0)
    first = owner_of(plan[places.ME], chips, d, other) * owned + low + at * block

    @pl.when(at == 0)
    def _():
        start = jnp.int32(0)
        for owner, count in ([(0, owned)] if other else []) + [(other, low)]:
            ahead = owner_of(plan[places.ME], chips, d, owner) * owned

            def add(j, total):
                return total + plan[places.steps + ahead + j]

            start = lax.fori_loop(0, count, add, start)
        offset[0] = members * start
        for c in range(tiles):
            below_rows[c, :capacity, :] = below[:, span(c)].astype(F32)
            below_rows[c, capacity:, :] = jnp.zeros((ROWS, LANES), F32)
            above_rows[c, ROWS:, :] = above[:, span(c)].astype(F32)
            above_rows[c, :ROWS, :] = jnp.zeros((ROWS, LANES), F32)

    def emit(j, c, values):
        smooth = [value.astype(BF16).astype(F32) for value in values]
        for v in range(out.shape[1]):
            total = None
            for m in range(members):
                term = pert[m, j, v, :, span(c)].astype(F32) * smooth[m]
                total = term if total is None else total + term
            if with_part:
                total = total + extra[0][j, v, :, span(c)].astype(F32)
            if with_variance:
                total = total + extra[0][j, v, :, span(c)] * grad[j, v, :, span(c)].astype(F32)
            out[j, v, :, span(c)] = total.astype(out.dtype)

    def one_level(j, carry):
        level = first + j
        count = plan[places.steps + level]
        rank = plan[places.ranks + level]

        @pl.when(rank >= top)
        def _():
            for m in range(members):
                off = jnp.minimum(offset[0], capacity)
                for c in range(tiles):
                    field[m, c, :ROWS, :] = above_rows[c, pl.ds(capacity - off, ROWS), :]
                    field[m, c, ROWS:2 * ROWS, :] = product_of(pert, grad, m, j, c).astype(F32)
                    field[m, c, 2 * ROWS:, :] = below_rows[c, pl.ds(off, ROWS), :]
                offset[0] = off + count

            def step(i, carry):
                for m in range(members):
                    sweep(field, keep, mix, m, ROWS - EDGE, ROWS + 2 * EDGE)
                return carry

            lax.fori_loop(1, count, step, 0)
            last = [diffuse_columns(field, keep, mix, m, ROWS, ROWS, EDGE) for m in range(members)]
            for c, values in enumerate(zip(*last)):
                emit(j, c, values)

        @pl.when(rank < top)
        def _():
            for c in range(tiles):
                if with_deep:
                    spots = [deep_place(rank * members + m, deep.shape[0], per_device) for m in range(members)]
                    emit(j, c, [deep[spot, :, span(c)] for spot in spots])
                else:
                    emit(j, c, [jnp.zeros((ROWS, LANES), F32)] * members)

        return carry

    lax.fori_loop(0, block, one_level, 0)


def smooth_owner(places, chips, d, other, low, count, top, per_device, plan, pert, grad, halos, keep, mix, deep, part, variance, block, dtype):
    members, _, variables, rows, cells = pert.shape
    tiles = cells // LANES
    capacity = halos[0].shape[0]
    owned = grad.shape[0]
    wholes = [halos[0], halos[1], keep, mix] + ([] if deep is None else [deep])
    extra = [x for x in (part, variance) if x is not None]
    kernel = functools.partial(
        smooth_kernel, places, chips, d, other, low, owned, top, per_device, deep is not None, part is not None, variance is not None
    )

    def whole(x):
        return pl.BlockSpec(x.shape, lambda i, *refs: (0,) * x.ndim)

    def pert_place(i, plan):
        return (0, owner_of(plan[places.ME], chips, d, other) * (owned // block) + low // block + i, 0, 0, 0)

    def levels_from(start):
        return pl.BlockSpec((block, variables, rows, cells), lambda i, *refs: (start // block + i, 0, 0, 0))

    return pl.pallas_call(
        kernel,
        out_shape=jax.ShapeDtypeStruct((count,) + grad.shape[1:], dtype),
        grid_spec=pltpu.PrefetchScalarGridSpec(
            num_scalar_prefetch=1,
            grid=(count // block,),
            in_specs=[pl.BlockSpec((members, block, variables, rows, cells), pert_place), levels_from(low)]
            + [whole(x) for x in wholes]
            + [levels_from(0) for x in extra],
            out_specs=levels_from(0),
            scratch_shapes=[
                pltpu.VMEM((tiles, capacity + ROWS, LANES), F32),
                pltpu.VMEM((tiles, capacity + ROWS, LANES), F32),
                pltpu.VMEM((members, tiles, 3 * ROWS, LANES), F32),
                pltpu.SMEM((1,), I32),
            ],
        ),
        compiler_params=pltpu.CompilerParams(vmem_limit_bytes=VMEM_BYTES),
        cost_estimate=cost(100 * grad.size, grad.size * 2 * (members + 3)),
    )(plan, pert, grad, *wholes, *extra)


def final_kernel(places, top, per_device, owned, parts, plan, pert, near, part, deep, *rest):
    arrived, out = rest[:-1], rest[-1]
    members, block = pert.shape[:2]
    at = pl.program_id(0)
    steps = pl.num_programs(0)
    first = plan[places.ME] * owned + at * block

    def total_of(j, v, c):
        total = near[j, v, :, span(c)] + part[j, v, :, span(c)].astype(F32)
        for d in range(0, len(arrived), parts):
            value = arrived[d][j, v, :, span(c)]
            for p in range(1, parts):
                value = jnp.where(at >= p * steps // parts, arrived[d + p][j, v, :, span(c)], value)
            total = total + value.astype(F32)
        return total

    for j in range(block):
        rank = plan[places.ranks + first + j]
        for v in range(out.shape[1]):
            for c in range(out.shape[3] // LANES):
                out[j, v, :, span(c)] = total_of(j, v, c)

        @pl.when(rank < top)
        def _():
            for c in range(out.shape[3] // LANES):
                smooth = [deep[deep_place(rank * members + m, deep.shape[0], per_device), :, span(c)].astype(F32) for m in range(members)]
                for v in range(out.shape[1]):
                    total = out[j, v, :, span(c)]
                    for m in range(members):
                        total = total + pert[m, j, v, :, span(c)].astype(F32) * smooth[m]
                    out[j, v, :, span(c)] = total


def final_sum(places, top, per_device, parts, plan, pert, near, part, deep, arrived, block):
    members, _, variables, rows, cells = pert.shape
    owned = near.shape[0]
    steps = owned // block

    def levels_at(p):
        def where(i, plan):
            return (jnp.clip(i - p * steps // parts, 0, steps // parts - 1), 0, 0, 0)

        return pl.BlockSpec((block, variables, rows, cells), where)

    here = pl.BlockSpec((block, variables, rows, cells), lambda i, plan: (i, 0, 0, 0))
    return pl.pallas_call(
        functools.partial(final_kernel, places, top, per_device, owned, parts),
        out_shape=jax.ShapeDtypeStruct(near.shape, F32),
        grid_spec=pltpu.PrefetchScalarGridSpec(
            num_scalar_prefetch=1,
            grid=(steps,),
            in_specs=[
                pl.BlockSpec((members, block, variables, rows, cells), lambda i, plan: (0, plan[places.ME] * steps + i, 0, 0, 0)),
                here, here, pl.BlockSpec(deep.shape, lambda i, plan: (0, 0, 0)),
            ] + [levels_at(i % parts) for i in range(len(arrived))],
            out_specs=here,
        ),
        compiler_params=pltpu.CompilerParams(vmem_limit_bytes=VMEM_BYTES),
        cost_estimate=cost(4 * near.size, near.size * 12),
        name="final_sum",
    )(plan, pert, near, part, deep, *arrived)


def program(pert, gradient, variance, class_map, values, level_steps, top, capacity):
    members, levels, _, rows, cells = pert.shape
    mem_count = lax.axis_size("mem")
    tile_count = lax.axis_size("tile")
    owned = gradient.shape[0]
    block, smooth_block, parts = 4, 2, PARTS
    chips = mem_count // 2
    per_device = top * members // tile_count
    places = Plan(levels, top, per_device)

    def hop(value, d):
        return lax.ppermute(value, "mem", [(i, ((i // 2 + d) % chips) * 2 + i % 2) for i in range(mem_count)])

    def swap(value):
        return lax.ppermute(value, "mem", [(i, i ^ 1) for i in range(mem_count)])

    south = [(i + 1, i) for i in range(tile_count - 1)]
    north = [(i, i + 1) for i in range(tile_count - 1)]

    far = []
    for d in range(1, chips):
        far.append(hop(gradient, d))
    position = jnp.stack([lax.axis_index("mem"), lax.axis_index("tile"), jnp.int32(tile_count)])
    plan, keep, mix = make_plan(places, top, per_device, owned, members, capacity, position, level_steps, values, class_map, rows)
    grads, halos = [], []
    for d in range(chips):
        near = gradient if d == 0 else far[d - 1]
        other = swap(near)
        grads += [near, other]
        if top < levels:
            tops, bottoms = pack_halos(places, chips, d, plan, pert, near, other, block, capacity)
            below = lax.ppermute(tops, "tile", south)
            above = lax.ppermute(bottoms, "tile", north)
            halos.append((below, above))
        else:
            halos.append((jnp.zeros((16, cells), BF16),) * 2)

    deep = deep_products(places, chips, plan, pert, grads, top, per_device)
    deep = deep.reshape(tile_count, per_device, rows, cells)
    field = lax.all_to_all(deep, "tile", split_axis=0, concat_axis=0, tiled=True)
    field = deep_smooth(places, plan, field, class_map, values)
    deep = lax.all_to_all(field, "tile", split_axis=0, concat_axis=0, tiled=True).reshape(-1, rows, cells)

    def smooth(d, other, low, count, whole, part, var, dtype):
        return smooth_owner(
            places, chips, d, other, low, count, top, per_device, plan, pert, grads[2 * d + other], halos[d], keep, mix,
            whole, part, var, smooth_block, dtype
        )

    near_sum = smooth(0, 0, 0, owned, None, None, variance, F32)
    arrived = []
    size = owned // parts
    for d in range(1, chips):
        crossed = []
        for p in range(parts):
            other = smooth(d, 1, p * size, size, deep, None, None, BF16)
            crossed.append(swap(other))
        for p in range(parts):
            both = smooth(d, 0, p * size, size, deep, crossed[p], None, BF16)
            arrived.append(hop(both, chips - d))
    part = smooth(0, 1, 0, owned, deep, None, None, BF16)
    part = swap(part)

    return plan, near_sum, part, deep, arrived


def finish(places, top, per_device, pert, sums):
    plan, near, part, deep, arrived = sums
    return final_sum(places, top, per_device, PARTS, plan, pert, near, part, deep, arrived, 2)


def shards(perturbations, gradient, static_variance, level_steps, class_map, class_diffusivity):
    members, levels = perturbations.shape[:2]
    owned = gradient.shape[0]
    top = lax.axis_size("tile") // members
    capacity = (5 * members * owned + 15) // 16 * 16
    operands = (perturbations, gradient, static_variance, class_map, class_diffusivity, level_steps)
    tiles = lax.axis_size("tile")
    sums = program(*operands, top, capacity)

    def halo(sums, *operands):
        return finish(Plan(levels, top, top * members // tiles), top, top * members // tiles, operands[0], sums)

    def general(sums, *operands):
        per_device = levels * members // tiles
        return finish(Plan(levels, levels, per_device), levels, per_device, operands[0], program(*operands, levels, 16))

    return lax.cond(sums[0][Plan.FITS] > 0, halo, general, sums, *operands)


def solution(mesh):
    placed = (
        P("mem", None, None, "tile", None),
        P("mem", None, "tile", None),
        P("mem", None, "tile", None),
        P(),
        P(),
        P(),
    )
    return jax.shard_map(
        shards, mesh=mesh, in_specs=placed, out_specs=P("mem", None, "tile", None), check_vma=False
    )
```

```python
import functools
import jax
import jax.numpy as jnp
from jax import lax
from jax.experimental import pallas as pl
from jax.experimental.pallas import tpu as pltpu
from jax.sharding import PartitionSpec as P

F32 = jnp.float32
BF16 = jnp.bfloat16
I32 = jnp.int32
LANES = 128
ROWS = 8
EDGE = 4
PARTS = 2
VMEM_BYTES = 67043328
SMEM_SPEC = pl.BlockSpec(memory_space=pltpu.SMEM)
VMEM_SPEC = pl.BlockSpec(memory_space=pltpu.VMEM)
ANY_SPEC = pl.BlockSpec(memory_space=pl.ANY)


def cost(flops, size):
    return pl.CostEstimate(flops=int(flops), transcendentals=0, bytes_accessed=int(size))


def span(c):
    return slice(c * LANES, (c + 1) * LANES)


def diffuse_columns(field, keep, mix, index, first, rows, weight_first):
    tiles = field.shape[1]
    lane = lax.broadcasted_iota(I32, (rows, LANES), 1)
    first_lane = lane == 0
    last_lane = lane == LANES - 1

    def load(c):
        here = field[index, c, first:first + rows, :]
        beside = field[index, c, first - 1:first - 1 + rows, :] + field[index, c, first + 1:first + 1 + rows, :]
        line = 4.0 * here + beside
        return here, line, pltpu.roll(line, 1, axis=1), pltpu.roll(line, LANES - 1, axis=1)

    here, line, to_east, to_west = load(0)
    start_west = to_west
    before = load(tiles - 1)[2]
    for c in range(tiles):
        if c + 1 < tiles:
            there = load(c + 1)
            after = there[3]
        else:
            there, after = None, start_west
        west = jnp.where(first_lane, before, to_east)
        east = jnp.where(last_lane, after, to_west)
        across = 4.0 * line + (west + east)
        place = slice(weight_first, weight_first + rows)
        yield keep[c, place, :] * here + mix[c, place, :] * across
        if there is not None:
            before = to_east
            here, line, to_east, to_west = there


def sweep(field, keep, mix, index, first, rows):
    for c, value in enumerate(diffuse_columns(field, keep, mix, index, first, rows, 0)):
        field[index, c, first:first + rows, :] = value


def diffusivity_of(classes, values, valid=None):
    total = jnp.zeros(classes.shape, F32)
    for k in range(values.shape[0]):
        total = jnp.where(classes == k, values[k], total)
    return total if valid is None else jnp.where(valid, total, 0.0)


def store_weights(keep, mix, c, place, diffusivity):
    keep[c, place, :] = 1.0 - 6.0 * diffusivity
    mix[c, place, :] = diffusivity * (1.0 / 6.0)


class Plan:
    ME, TILE = 0, 1

    def __init__(self, levels, top, per_device):
        self.steps = 8
        self.ranks = self.steps + levels
        self.deep = self.ranks + levels
        self.mine = self.deep + top + 1
        self.size = self.mine + per_device


BINS = 16


def plan_kernel(places, top, per_device, owned, members, capacities, level_steps, plan, fits, bins, deep_steps):
    levels = level_steps.shape[0]
    me, tile, tile_count = lax.axis_index("mem"), lax.axis_index("tile"), lax.axis_size("tile")
    plan[places.ME] = me
    plan[places.TILE] = tile
    for i in range(2, places.steps):
        plan[i] = 0

    def bin_of(level):
        return jnp.clip(level_steps[level], 0, BINS - 1)

    for i in range(BINS):
        bins[i] = 0

    def count(level, carry):
        bins[bin_of(level)] += 1
        return carry

    lax.fori_loop(0, levels, count, 0)
    total = jnp.int32(0)
    for i in reversed(range(BINS)):
        here_count = bins[i]
        bins[i] = total
        total = total + here_count

    def assign(level, carry):
        chip_rows, owner_rows, fits = carry
        b = bin_of(level)
        rank = bins[b]
        bins[b] = rank + 1
        whole = rank < top
        steps = jnp.where(whole, 0, level_steps[level])
        plan[places.ranks + level] = rank
        plan[places.steps + level] = steps
        slot = jnp.minimum(rank, top)
        plan[places.deep + slot] = level
        deep_steps[slot] = level_steps[level]
        chip_rows = jnp.where(lax.rem(level, 2 * owned) == 0, 0, chip_rows) + members * steps
        owner_rows = jnp.where(lax.rem(level, owned) == 0, 0, owner_rows) + 2 * members * steps
        inside = (chip_rows <= capacities[0]) & (owner_rows <= capacities[1]) & (steps <= EDGE)
        return chip_rows, owner_rows, jnp.where(inside, fits, 0)

    fits[0] = lax.fori_loop(0, levels, assign, (jnp.int32(0), jnp.int32(0), jnp.int32(1)))[2]
    plan[places.deep + top] = 0
    for j in range(per_device):
        plan[places.mine + j] = deep_steps[(j * tile_count + tile) // members]


def make_plan(places, top, per_device, owned, members, capacities, level_steps):
    return pl.pallas_call(
        functools.partial(plan_kernel, places, top, per_device, owned, members, capacities),
        out_shape=(jax.ShapeDtypeStruct((places.size,), I32), jax.ShapeDtypeStruct((1,), I32)),
        in_specs=[SMEM_SPEC],
        out_specs=[SMEM_SPEC, SMEM_SPEC],
        scratch_shapes=[pltpu.SMEM((BINS,), I32), pltpu.SMEM((top + 1,), I32)],
        compiler_params=pltpu.CompilerParams(vmem_limit_bytes=VMEM_BYTES),
        cost_estimate=cost(0, 4 * places.size),
        name="plan",
    )(level_steps)


def weights_kernel(places, tile_count, plan, values, before, here, after, keep, mix):
    tile = plan[places.TILE]
    inside_before = jnp.broadcast_to(tile > 0, (ROWS, LANES))
    inside_after = jnp.broadcast_to(tile < tile_count - 1, (ROWS, LANES))
    for c in range(keep.shape[0]):
        upper = diffusivity_of(before[:, span(c)], values, inside_before)
        lower = diffusivity_of(after[:, span(c)], values, inside_after)
        store_weights(keep, mix, c, slice(0, EDGE), upper[ROWS - EDGE:])
        store_weights(keep, mix, c, slice(EDGE, EDGE + ROWS), diffusivity_of(here[:, span(c)], values))
        store_weights(keep, mix, c, slice(EDGE + ROWS, 2 * EDGE + ROWS), lower[:EDGE])


def make_weights(places, plan, values, class_map, rows):
    cells = class_map.shape[1]
    tiles = cells // LANES
    row_tiles = class_map.shape[0] // rows
    weights = jax.ShapeDtypeStruct((tiles, 2 * EDGE + rows, LANES), F32)
    weight_spec = pl.BlockSpec(weights.shape, lambda i, *refs: (0, 0, 0))

    def rows_at(shift):
        return pl.BlockSpec((rows, cells), lambda i, plan, *refs: (jnp.clip(plan[places.TILE] + shift, 0, row_tiles - 1), 0))

    return pl.pallas_call(
        functools.partial(weights_kernel, places, row_tiles),
        out_shape=(weights, weights),
        grid_spec=pltpu.PrefetchScalarGridSpec(
            num_scalar_prefetch=2,
            grid=(1,),
            in_specs=[rows_at(-1), rows_at(0), rows_at(1)],
            out_specs=[weight_spec, weight_spec],
        ),
        compiler_params=pltpu.CompilerParams(vmem_limit_bytes=VMEM_BYTES),
        cost_estimate=cost(0, 4 * weights.size * 2),
        name="weights",
    )(plan, values, class_map, class_map, class_map)


def owner_of(me, chips, d, other):
    return lax.rem(me // 2 - d + chips, chips) * 2 + lax.rem(me + other, 2)


def product_of(pert, grad, member, level, c):
    total = None
    for v in range(grad.shape[1]):
        term = pert[member, level, v, :, span(c)].astype(F32) * grad[level, v, :, span(c)].astype(F32)
        total = term if total is None else total + term
    return total.astype(BF16)


def pack_owners_kernel(places, chips, d, plan, pert, near, far, tops, bottoms, top_rows, bottom_rows, offset):
    members, block = pert.shape[:2]
    capacity = tops.shape[0]
    at = pl.program_id(0)
    half = pl.num_programs(0) // 2
    owned = half * block

    @pl.when(at == 0)
    def _():
        offset[0] = 0

    def pack(grad, other, i):
        first = owner_of(plan[places.ME], chips, d, other) * owned + i * block
        for j in range(block):
            count = plan[places.steps + first + j]
            for m in range(members):
                off = jnp.minimum(offset[0], capacity)
                for c in range(top_rows.shape[0]):
                    part = product_of(pert, grad, m, j, c).astype(F32)
                    top_rows[c, pl.ds(off, ROWS), :] = part
                    bottom_rows[c, pl.ds(capacity - off, ROWS), :] = part
                offset[0] = off + count

    @pl.when(at < half)
    def _():
        pack(near, 0, at)

    @pl.when(at >= half)
    def _():
        pack(far, 1, at - half)

    @pl.when(at == 2 * half - 1)
    def _():
        for c in range(top_rows.shape[0]):
            tops[:, span(c)] = top_rows[c, :capacity, :].astype(BF16)
            bottoms[:, span(c)] = bottom_rows[c, ROWS:, :].astype(BF16)


def pack_owners(places, chips, d, plan, pert, near, far, block, capacity):
    members, _, variables, rows, cells = pert.shape
    blocks = near.shape[0] // block
    out = jax.ShapeDtypeStruct((capacity, cells), BF16)
    whole = pl.BlockSpec((capacity, cells), lambda i, plan: (0, 0))
    grad_block = (block, variables, rows, cells)

    def pert_place(i, plan):
        other = i // blocks
        return (0, owner_of(plan[places.ME], chips, d, other) * blocks + lax.rem(i, blocks), 0, 0, 0)

    return pl.pallas_call(
        functools.partial(pack_owners_kernel, places, chips, d),
        out_shape=(out, out),
        grid_spec=pltpu.PrefetchScalarGridSpec(
            num_scalar_prefetch=1,
            grid=(2 * blocks,),
            in_specs=[
                pl.BlockSpec((members,) + grad_block, pert_place),
                pl.BlockSpec(grad_block, lambda i, plan: (jnp.minimum(i, blocks - 1), 0, 0, 0)),
                pl.BlockSpec(grad_block, lambda i, plan: (jnp.maximum(i - blocks, 0), 0, 0, 0)),
            ],
            out_specs=[whole, whole],
            scratch_shapes=[
                pltpu.VMEM((cells // LANES, capacity + ROWS, LANES), F32),
                pltpu.VMEM((cells // LANES, capacity + ROWS, LANES), F32),
                pltpu.SMEM((1,), I32),
            ],
        ),
        compiler_params=pltpu.CompilerParams(vmem_limit_bytes=VMEM_BYTES),
        cost_estimate=cost(8 * near.size, 2 * near.size * 2 * (members + 1)),
    )(plan, pert, near, far)


def pack_members_kernel(places, chips, d, plan, pert, mate, grad, tops, bottoms, top_rows, bottom_rows, offset):
    members, block = pert.shape[:2]
    capacity = tops.shape[0]
    at = pl.program_id(0)
    owned = pl.num_programs(0) * block
    first = owner_of(plan[places.ME], chips, d, 0) * owned + at * block

    @pl.when(at == 0)
    def _():
        offset[0] = 0

    for j in range(block):
        count = plan[places.steps + first + j]
        for source in (pert, mate):
            for m in range(members):
                off = jnp.minimum(offset[0], capacity)
                for c in range(top_rows.shape[0]):
                    part = product_of(source, grad, m, j, c).astype(F32)
                    top_rows[c, pl.ds(off, ROWS), :] = part
                    bottom_rows[c, pl.ds(capacity - off, ROWS), :] = part
                offset[0] = off + count

    @pl.when(at == pl.num_programs(0) - 1)
    def _():
        for c in range(top_rows.shape[0]):
            tops[:, span(c)] = top_rows[c, :capacity, :].astype(BF16)
            bottoms[:, span(c)] = bottom_rows[c, ROWS:, :].astype(BF16)


def pack_members(places, chips, d, plan, pert, mate, grad, block, capacity):
    members, _, variables, rows, cells = pert.shape
    blocks = grad.shape[0] // block
    out = jax.ShapeDtypeStruct((capacity, cells), BF16)
    whole = pl.BlockSpec((capacity, cells), lambda i, plan: (0, 0))
    pert_block = (members, block, variables, rows, cells)

    def pert_place(i, plan):
        return (0, owner_of(plan[places.ME], chips, d, 0) * blocks + i, 0, 0, 0)

    return pl.pallas_call(
        functools.partial(pack_members_kernel, places, chips, d),
        out_shape=(out, out),
        grid_spec=pltpu.PrefetchScalarGridSpec(
            num_scalar_prefetch=1,
            grid=(blocks,),
            in_specs=[
                pl.BlockSpec(pert_block, pert_place),
                pl.BlockSpec(pert_block, lambda i, plan: (0, i, 0, 0, 0)),
                pl.BlockSpec(pert_block[1:], lambda i, plan: (i, 0, 0, 0)),
            ],
            out_specs=[whole, whole],
            scratch_shapes=[
                pltpu.VMEM((cells // LANES, capacity + ROWS, LANES), F32),
                pltpu.VMEM((cells // LANES, capacity + ROWS, LANES), F32),
                pltpu.SMEM((1,), I32),
            ],
        ),
        compiler_params=pltpu.CompilerParams(vmem_limit_bytes=VMEM_BYTES),
        cost_estimate=cost(16 * grad.size, grad.size * 2 * (2 * members + 1)),
    )(plan, pert, mate, grad)


def deep_product_kernel(places, chips, per_device, group, plan, *refs):
    perts, grads, out = refs[:group], refs[group:-1], refs[-1]
    members = perts[0].shape[0]
    count = len(grads) // group

    for u in range(group):
        k = pl.program_id(0) * group + u
        pert = perts[u]
        place = grad_place(places, chips, count, plan, k)[0]

        def form(grad):
            for m in range(members):
                spot = deep_place(k * members + m, out.shape[0], per_device)
                for c in range(pert.shape[-1] // LANES):
                    out[spot, :, span(c)] = product_of(pert, grad, m, 0, c)

        for g in range(count):
            pl.when(place == g)(functools.partial(form, grads[u * count + g]))


def grad_place(places, chips, count, plan, k):
    levels = places.ranks - places.steps
    owned = levels // count
    level = plan[places.deep + k]
    owner = level // owned
    shift = lax.rem(plan[places.ME] // 2 - owner // 2 + chips, chips)
    return 2 * shift + lax.rem(plan[places.ME] + owner, 2), lax.rem(level, owned)


def deep_products(places, chips, plan, pert, grads, top, per_device):
    members, _, variables, rows, cells = pert.shape
    group = 4 if top == 4 else 1

    def pert_spec(u):
        return pl.BlockSpec((members, 1, variables, rows, cells), lambda i, plan: (0, plan[places.deep + i * group + u], 0, 0, 0))

    def grad_spec(u, g):
        def where(i, plan):
            place, level = grad_place(places, chips, len(grads), plan, i * group + u)
            return (jnp.where(place == g, level, 0), 0, 0, 0)

        return pl.BlockSpec((1, variables, rows, cells), where)

    return pl.pallas_call(
        functools.partial(deep_product_kernel, places, chips, per_device, group),
        out_shape=jax.ShapeDtypeStruct((top * members, rows, cells), BF16),
        grid_spec=pltpu.PrefetchScalarGridSpec(
            num_scalar_prefetch=1,
            grid=(top // group,),
            in_specs=[pert_spec(u) for u in range(group)] + [grad_spec(u, g) for u in range(group) for g in range(len(grads))],
            out_specs=pl.BlockSpec((top * members, rows, cells), lambda i, plan: (0, 0, 0)),
        ),
        compiler_params=pltpu.CompilerParams(vmem_limit_bytes=VMEM_BYTES),
        cost_estimate=cost(top * members * rows * cells * 4, top * members * rows * cells * 8),
        name="deep_product",
    )(plan, *([pert] * group), *(list(grads) * group))


def deep_kernel(mine, plan, values, planes, class_map, out, field, keep, mix):
    at = pl.program_id(0)
    parts, _, rows, _ = planes.shape
    height = parts * rows
    tiles = field.shape[1]

    @pl.when(at == 0)
    def _():
        for c in range(tiles):
            field[0, c, :ROWS, :] = jnp.zeros((ROWS, LANES), F32)
            field[0, c, ROWS + height:, :] = jnp.zeros((ROWS, LANES), F32)
            store_weights(keep, mix, c, slice(0, height), diffusivity_of(class_map[:, span(c)], values))

    for p in range(parts):
        for c in range(tiles):
            field[0, c, ROWS + p * rows:ROWS + (p + 1) * rows, :] = planes[p, 0, :, span(c)].astype(F32)

    def step(i, carry):
        sweep(field, keep, mix, 0, ROWS, height)
        return carry

    lax.fori_loop(0, plan[mine + at], step, 0)
    for p in range(parts):
        for c in range(tiles):
            out[p, 0, :, span(c)] = field[0, c, ROWS + p * rows:ROWS + (p + 1) * rows, :].astype(BF16)


def deep_smooth(places, plan, planes, class_map, values):
    parts, per_device, rows, cells = planes.shape
    tiles = cells // LANES
    plane = pl.BlockSpec((parts, 1, rows, cells), lambda i: (0, i, 0, 0))
    return pl.pallas_call(
        functools.partial(deep_kernel, places.mine),
        out_shape=jax.ShapeDtypeStruct(planes.shape, BF16),
        grid=(per_device,),
        in_specs=[SMEM_SPEC, SMEM_SPEC, plane, VMEM_SPEC],
        out_specs=plane,
        scratch_shapes=[
            pltpu.VMEM((1, tiles, parts * rows + 2 * ROWS, LANES), F32),
            pltpu.VMEM((tiles, parts * rows, LANES), F32),
            pltpu.VMEM((tiles, parts * rows, LANES), F32),
        ],
        compiler_params=pltpu.CompilerParams(vmem_limit_bytes=VMEM_BYTES),
        cost_estimate=cost(150 * planes.size, planes.size * 4 + parts * rows * cells * 4),
        name="deep_smooth",
    )(plan, values, planes, class_map)


def deep_place(q, planes, per_device):
    devices = planes // per_device
    return lax.rem(q, devices) * per_device + q // devices


def smooth_kernel(places, chips, d, other, low, owned, top, per_device, with_mate, deep_count, with_variance, plan, pert, grad, below, above, keep, mix, *rest):
    extra, (out, below_rows, above_rows, field, offset) = rest[:-5], rest[-5:]
    perts = (pert,)
    if with_mate:
        perts, extra = (pert, extra[0]), extra[1:]
    deeps, extra = extra[:deep_count], extra[deep_count:]
    members, block = pert.shape[:2]
    sources = [(source, m) for source in perts for m in range(members)]
    capacity = below.shape[0]
    tiles = field.shape[1]
    at = pl.program_id(0)
    ahead = owner_of(plan[places.ME], chips, d, other) * owned

    @pl.when(at == 0)
    def _():
        start = jnp.int32(0)
        for owner, count in ([(0, owned)] if other else []) + [(other, low)]:
            base = places.steps + owner_of(plan[places.ME], chips, d, owner) * owned

            def add(j, total):
                return total + plan[base + j]

            start = lax.fori_loop(0, count, add, start)
        offset[0] = len(sources) * start
        for c in range(tiles):
            below_rows[c, :capacity, :] = below[:, span(c)].astype(F32)
            below_rows[c, capacity:, :] = jnp.zeros((ROWS, LANES), F32)
            above_rows[c, ROWS:, :] = above[:, span(c)].astype(F32)
            above_rows[c, :ROWS, :] = jnp.zeros((ROWS, LANES), F32)

    def emit(j, c, values):
        smooth = [value.astype(BF16).astype(F32) for value in values]
        for v in range(out.shape[1]):
            total = None
            for (source, m), value in zip(sources, smooth):
                term = source[m, j, v, :, span(c)].astype(F32) * value
                total = term if total is None else total + term
            if with_variance:
                total = total + extra[0][j, v, :, span(c)] * grad[j, v, :, span(c)].astype(F32)
            out[j, v, :, span(c)] = total.astype(out.dtype)

    def one_level(j, carry):
        level = ahead + low + at * block + j
        count = plan[places.steps + level]
        rank = plan[places.ranks + level]

        @pl.when(rank >= top)
        def _():
            for i, (source, m) in enumerate(sources):
                off = jnp.minimum(offset[0], capacity)
                for c in range(tiles):
                    field[i, c, :ROWS, :] = above_rows[c, pl.ds(capacity - off, ROWS), :]
                    field[i, c, ROWS:2 * ROWS, :] = product_of(source, grad, m, j, c).astype(F32)
                    field[i, c, 2 * ROWS:, :] = below_rows[c, pl.ds(off, ROWS), :]
                offset[0] = off + count

            def step(i, carry):
                for i in range(len(sources)):
                    sweep(field, keep, mix, i, ROWS - EDGE, ROWS + 2 * EDGE)
                return carry

            lax.fori_loop(1, count, step, 0)
            last = [diffuse_columns(field, keep, mix, i, ROWS, ROWS, EDGE) for i in range(len(sources))]
            for c, values in enumerate(zip(*last)):
                emit(j, c, values)

        @pl.when(rank < top)
        def _():
            for c in range(tiles):
                if deep_count > 0:
                    spots = [deep_place(rank * members + m, deeps[0].shape[0], per_device) for m in range(members)]
                    emit(j, c, [deep[spot, :, span(c)] for deep in deeps for spot in spots])
                else:
                    emit(j, c, [jnp.zeros((ROWS, LANES), F32)] * len(sources))

        return carry

    lax.fori_loop(0, block, one_level, 0)


def smooth_owner(places, chips, d, other, low, count, top, per_device, plan, pert, mate, grad, halos, keep, mix, deeps, variance, block, dtype):
    members, _, variables, rows, cells = pert.shape
    tiles = cells // LANES
    capacity = halos[0].shape[0]
    owned = grad.shape[0]
    mates = [] if mate is None else [mate]
    extra = [] if variance is None else [variance]
    kernel = functools.partial(
        smooth_kernel, places, chips, d, other, low, owned, top, per_device, mate is not None, len(deeps), variance is not None
    )

    def whole(x):
        return pl.BlockSpec(x.shape, lambda i, *refs: (0,) * x.ndim)

    def pert_place(i, plan):
        return (0, owner_of(plan[places.ME], chips, d, other) * (owned // block) + low // block + i, 0, 0, 0)

    def levels_from(start):
        return pl.BlockSpec((block, variables, rows, cells), lambda i, *refs: (start // block + i, 0, 0, 0))

    pert_block = (members, block, variables, rows, cells)
    return pl.pallas_call(
        kernel,
        out_shape=jax.ShapeDtypeStruct((count,) + grad.shape[1:], dtype),
        grid_spec=pltpu.PrefetchScalarGridSpec(
            num_scalar_prefetch=1,
            grid=(count // block,),
            in_specs=[pl.BlockSpec(pert_block, pert_place), levels_from(low)]
            + [whole(x) for x in (halos[0], halos[1], keep, mix)]
            + [pl.BlockSpec(pert_block, lambda i, plan: (0, low // block + i, 0, 0, 0)) for x in mates]
            + [whole(x) for x in deeps]
            + [levels_from(low) for x in extra],
            out_specs=levels_from(0),
            scratch_shapes=[
                pltpu.VMEM((tiles, capacity + ROWS, LANES), F32),
                pltpu.VMEM((tiles, capacity + ROWS, LANES), F32),
                pltpu.VMEM(((1 + len(mates)) * members, tiles, 3 * ROWS, LANES), F32),
                pltpu.SMEM((1,), I32),
            ],
        ),
        compiler_params=pltpu.CompilerParams(vmem_limit_bytes=VMEM_BYTES),
        cost_estimate=cost(100 * grad.size, grad.size * 2 * (members + 3)),
    )(plan, pert, grad, halos[0], halos[1], keep, mix, *mates, *deeps, *extra)


def final_kernel(places, top, per_device, owned, parts, plan, pert, near, part, deep, *rest):
    arrived, out = rest[:-1], rest[-1]
    members, block = pert.shape[:2]
    at = pl.program_id(0)
    steps = pl.num_programs(0)
    first = plan[places.ME] * owned + at * block

    def total_of(j, v, c):
        total = near[j, v, :, span(c)] + part[j, v, :, span(c)].astype(F32)
        for d in range(0, len(arrived), parts):
            value = arrived[d][j, v, :, span(c)]
            for p in range(1, parts):
                value = jnp.where(at >= p * steps // parts, arrived[d + p][j, v, :, span(c)], value)
            total = total + value.astype(F32)
        return total

    for j in range(block):
        rank = plan[places.ranks + first + j]
        for v in range(out.shape[1]):
            for c in range(out.shape[3] // LANES):
                out[j, v, :, span(c)] = total_of(j, v, c)

        @pl.when(rank < top)
        def _():
            for c in range(out.shape[3] // LANES):
                smooth = [deep[deep_place(rank * members + m, deep.shape[0], per_device), :, span(c)].astype(F32) for m in range(members)]
                for v in range(out.shape[1]):
                    total = out[j, v, :, span(c)]
                    for m in range(members):
                        total = total + pert[m, j, v, :, span(c)].astype(F32) * smooth[m]
                    out[j, v, :, span(c)] = total


def final_sum(places, top, per_device, parts, plan, pert, near, part, deep, arrived, block):
    members, _, variables, rows, cells = pert.shape
    owned = near.shape[0]
    steps = owned // block

    def levels_at(p):
        def where(i, plan):
            return (jnp.clip(i - p * steps // parts, 0, steps // parts - 1), 0, 0, 0)

        return pl.BlockSpec((block, variables, rows, cells), where)

    here = pl.BlockSpec((block, variables, rows, cells), lambda i, plan: (i, 0, 0, 0))
    return pl.pallas_call(
        functools.partial(final_kernel, places, top, per_device, owned, parts),
        out_shape=jax.ShapeDtypeStruct(near.shape, F32),
        grid_spec=pltpu.PrefetchScalarGridSpec(
            num_scalar_prefetch=1,
            grid=(steps,),
            in_specs=[
                pl.BlockSpec((members, block, variables, rows, cells), lambda i, plan: (0, plan[places.ME] * steps + i, 0, 0, 0)),
                here, here, pl.BlockSpec(deep.shape, lambda i, plan: (0, 0, 0)),
            ] + [levels_at(i % parts) for i in range(len(arrived))],
            out_specs=here,
        ),
        compiler_params=pltpu.CompilerParams(vmem_limit_bytes=VMEM_BYTES),
        cost_estimate=cost(4 * near.size, near.size * 12),
        name="final_sum",
    )(plan, pert, near, part, deep, *arrived)


def program(pert, gradient, variance, class_map, values, level_steps, top, capacities):
    members, levels, _, rows, cells = pert.shape
    mem_count = lax.axis_size("mem")
    tile_count = lax.axis_size("tile")
    owned = gradient.shape[0]
    chips = mem_count // 2
    per_device = top * members // tile_count
    places = Plan(levels, top, per_device)

    def hop(value, d):
        return lax.ppermute(value, "mem", [(i, ((i // 2 + d) % chips) * 2 + i % 2) for i in range(mem_count)])

    def swap(value):
        return lax.ppermute(value, "mem", [(i, i ^ 1) for i in range(mem_count)])

    south = [(i + 1, i) for i in range(tile_count - 1)]
    north = [(i, i + 1) for i in range(tile_count - 1)]

    grads = [gradient]
    for d in range(1, chips):
        grads.append(hop(gradient, d))
    me = lax.axis_index("mem")
    plan, fits = make_plan(places, top, per_device, owned, members, capacities, level_steps)
    keep, mix = make_weights(places, plan, values, class_map, rows)
    fits = fits[0] > 0
    mates = [None]
    for d in range(1, chips):
        mates.append(swap(lax.dynamic_slice_in_dim(pert, owner_of(me, chips, d, 1) * owned, owned, axis=1)))
    halos, both_grads = [], []
    for d in range(chips):
        other = swap(grads[d])
        both_grads += [grads[d], other]
        if top < levels:
            if d == 0:
                tops, bottoms = pack_owners(places, chips, d, plan, pert, gradient, other, min(8, owned), capacities[0])
            else:
                tops, bottoms = pack_members(places, chips, d, plan, pert, mates[d], grads[d], min(4, owned), capacities[1])
            below = lax.ppermute(tops, "tile", south)
            above = lax.ppermute(bottoms, "tile", north)
            halos.append((below, above))
        else:
            halos.append((jnp.zeros((16, cells), BF16),) * 2)

    deep = deep_products(places, chips, plan, pert, both_grads, top, per_device)
    deep = deep.reshape(tile_count, per_device, rows, cells)
    field = lax.all_to_all(deep, "tile", split_axis=0, concat_axis=0, tiled=True)
    field = deep_smooth(places, plan, field, class_map, values)
    deep = lax.all_to_all(field, "tile", split_axis=0, concat_axis=0, tiled=True).reshape(-1, rows, cells)
    deeps = (deep, swap(deep))

    def smooth(d, other, low, size, whole, var, dtype):
        return smooth_owner(
            places, chips, d, other, low, size, top, per_device, plan, pert, mates[d], both_grads[2 * d + other], halos[d], keep, mix,
            whole, var, min(4, size), dtype
        )

    near = smooth(0, 0, 0, owned, (), variance, F32)
    arrived = []
    size = owned // PARTS
    for d in range(1, chips):
        for p in range(PARTS):
            part = smooth(d, 0, p * size, size, deeps, None, BF16)
            arrived.append(hop(part, chips - d))
    part = smooth(0, 1, 0, owned, deeps[:1], None, BF16)
    part = swap(part)
    return fits, (plan, near, part, deep, arrived)


def finish(places, top, per_device, pert, sums):
    plan, near, part, deep, arrived = sums
    return final_sum(places, top, per_device, PARTS, plan, pert, near, part, deep, arrived, min(4, near.shape[0] // PARTS))


def shards(perturbations, gradient, static_variance, level_steps, class_map, class_diffusivity):
    members, levels = perturbations.shape[:2]
    owned = gradient.shape[0]
    top = lax.axis_size("tile") // members
    capacities = ((5 * members * owned + 7) // 8 * 8, (11 * members * owned // 2 + 7) // 8 * 8)
    operands = (perturbations, gradient, static_variance, class_map, class_diffusivity, level_steps)
    tiles = lax.axis_size("tile")
    fits, sums = program(*operands, top, capacities)

    def halo(sums, *operands):
        return finish(Plan(levels, top, top * members // tiles), top, top * members // tiles, operands[0], sums)

    def general(sums, *operands):
        per_device = levels * members // tiles
        return finish(Plan(levels, levels, per_device), levels, per_device, operands[0], program(*operands, levels, (0, 0))[1])

    return lax.cond(fits, halo, general, sums, *operands)


def solution(mesh):
    placed = (
        P("mem", None, None, "tile", None),
        P("mem", None, "tile", None),
        P("mem", None, "tile", None),
        P(),
        P(),
        P(),
    )
    return jax.shard_map(
        shards, mesh=mesh, in_specs=placed, out_specs=P("mem", None, "tile", None), check_vma=False
    )
```

```python
import functools
import jax
import jax.numpy as jnp
from jax import lax
from jax.experimental import pallas as pl
from jax.experimental.pallas import tpu as pltpu
from jax.sharding import PartitionSpec as P

F32 = jnp.float32
BF16 = jnp.bfloat16
I32 = jnp.int32
LANES = 128
ROWS = 8
EDGE = 4
PARTS = 2
VMEM_BYTES = 32 * 1024 * 1024
SMEM_SPEC = pl.BlockSpec(memory_space=pltpu.SMEM)
VMEM_SPEC = pl.BlockSpec(memory_space=pltpu.VMEM)
ANY_SPEC = pl.BlockSpec(memory_space=pl.ANY)


def cost(flops, size):
    return pl.CostEstimate(flops=int(flops), transcendentals=0, bytes_accessed=int(size))


def span(c):
    return slice(c * LANES, (c + 1) * LANES)


def diffuse_columns(field, keep, mix, index, first, rows, weight_first):
    tiles = field.shape[1]
    lane = lax.broadcasted_iota(I32, (rows, LANES), 1)
    first_lane = lane == 0
    last_lane = lane == LANES - 1

    def load(c):
        here = field[index, c, first:first + rows, :]
        beside = field[index, c, first - 1:first - 1 + rows, :] + field[index, c, first + 1:first + 1 + rows, :]
        line = 4.0 * here + beside
        return here, line, pltpu.roll(line, 1, axis=1), pltpu.roll(line, LANES - 1, axis=1)

    here, line, to_east, to_west = load(0)
    start_west = to_west
    before = load(tiles - 1)[2]
    for c in range(tiles):
        if c + 1 < tiles:
            there = load(c + 1)
            after = there[3]
        else:
            there, after = None, start_west
        west = jnp.where(first_lane, before, to_east)
        east = jnp.where(last_lane, after, to_west)
        across = 4.0 * line + (west + east)
        place = slice(weight_first, weight_first + rows)
        yield keep[c, place, :] * here + mix[c, place, :] * across
        if there is not None:
            before = to_east
            here, line, to_east, to_west = there


def sweep(field, keep, mix, index, first, rows):
    for c, value in enumerate(diffuse_columns(field, keep, mix, index, first, rows, 0)):
        field[index, c, first:first + rows, :] = value


def diffusivity_of(classes, values, valid=None):
    total = jnp.zeros(classes.shape, F32)
    for k in range(values.shape[0]):
        total = jnp.where(classes == k, values[k], total)
    return total if valid is None else jnp.where(valid, total, 0.0)


def store_weights(keep, mix, c, place, diffusivity):
    keep[c, place, :] = 1.0 - 6.0 * diffusivity
    mix[c, place, :] = diffusivity * (1.0 / 6.0)


class Plan:
    ME, TILE = 0, 1

    def __init__(self, levels, top, per_device):
        self.steps = 8
        self.ranks = self.steps + levels
        self.deep = self.ranks + levels
        self.mine = self.deep + top + 1
        self.size = self.mine + per_device


BINS = 16


def plan_kernel(places, top, per_device, owned, members, capacities, level_steps, plan, fits, bins, deep_steps):
    levels = level_steps.shape[0]
    me, tile, tile_count = lax.axis_index("mem"), lax.axis_index("tile"), lax.axis_size("tile")
    plan[places.ME] = me
    plan[places.TILE] = tile
    for i in range(2, places.steps):
        plan[i] = 0

    def bin_of(level):
        return jnp.clip(level_steps[level], 0, BINS - 1)

    for i in range(BINS):
        bins[i] = 0

    def count(level, carry):
        bins[bin_of(level)] += 1
        return carry

    lax.fori_loop(0, levels, count, 0, unroll=4)
    total = jnp.int32(0)
    for i in reversed(range(BINS)):
        here_count = bins[i]
        bins[i] = total
        total = total + here_count

    def assign(level, carry):
        chip_rows, owner_rows, fits = carry
        b = bin_of(level)
        rank = bins[b]
        bins[b] = rank + 1
        whole = rank < top
        steps = jnp.where(whole, 0, level_steps[level])
        plan[places.ranks + level] = rank
        plan[places.steps + level] = steps
        slot = jnp.minimum(rank, top)
        plan[places.deep + slot] = level
        deep_steps[slot] = level_steps[level]
        chip_rows = jnp.where(lax.rem(level, 2 * owned) == 0, 0, chip_rows) + members * steps
        owner_rows = jnp.where(lax.rem(level, owned) == 0, 0, owner_rows) + 2 * members * steps
        inside = (chip_rows <= capacities[0]) & (owner_rows <= capacities[1]) & (steps <= EDGE)
        return chip_rows, owner_rows, jnp.where(inside, fits, 0)

    fits[0] = lax.fori_loop(0, levels, assign, (jnp.int32(0), jnp.int32(0), jnp.int32(1)), unroll=4)[2]
    plan[places.deep + top] = 0
    for j in range(per_device):
        plan[places.mine + j] = deep_steps[(j * tile_count + tile) // members]


def make_plan(places, top, per_device, owned, members, capacities, level_steps):
    return pl.pallas_call(
        functools.partial(plan_kernel, places, top, per_device, owned, members, capacities),
        out_shape=(jax.ShapeDtypeStruct((places.size,), I32), jax.ShapeDtypeStruct((1,), I32)),
        in_specs=[SMEM_SPEC],
        out_specs=[SMEM_SPEC, SMEM_SPEC],
        scratch_shapes=[pltpu.SMEM((BINS,), I32), pltpu.SMEM((top + 1,), I32)],
        compiler_params=pltpu.CompilerParams(vmem_limit_bytes=VMEM_BYTES),
        cost_estimate=cost(0, 4 * places.size),
        name="plan",
    )(level_steps)


def weights_kernel(places, tile_count, plan, values, before, here, after, keep, mix):
    tile = plan[places.TILE]
    inside_before = jnp.broadcast_to(tile > 0, (ROWS, LANES))
    inside_after = jnp.broadcast_to(tile < tile_count - 1, (ROWS, LANES))
    for c in range(keep.shape[0]):
        upper = diffusivity_of(before[:, span(c)], values, inside_before)
        lower = diffusivity_of(after[:, span(c)], values, inside_after)
        store_weights(keep, mix, c, slice(0, EDGE), upper[ROWS - EDGE:])
        store_weights(keep, mix, c, slice(EDGE, EDGE + ROWS), diffusivity_of(here[:, span(c)], values))
        store_weights(keep, mix, c, slice(EDGE + ROWS, 2 * EDGE + ROWS), lower[:EDGE])


def make_weights(places, plan, values, class_map, rows):
    cells = class_map.shape[1]
    tiles = cells // LANES
    row_tiles = class_map.shape[0] // rows
    weights = jax.ShapeDtypeStruct((tiles, 2 * EDGE + rows, LANES), F32)
    weight_spec = pl.BlockSpec(weights.shape, lambda i, *refs: (0, 0, 0))

    def rows_at(shift):
        return pl.BlockSpec((rows, cells), lambda i, plan, *refs: (jnp.clip(plan[places.TILE] + shift, 0, row_tiles - 1), 0))

    return pl.pallas_call(
        functools.partial(weights_kernel, places, row_tiles),
        out_shape=(weights, weights),
        grid_spec=pltpu.PrefetchScalarGridSpec(
            num_scalar_prefetch=2,
            grid=(1,),
            in_specs=[rows_at(-1), rows_at(0), rows_at(1)],
            out_specs=[weight_spec, weight_spec],
        ),
        compiler_params=pltpu.CompilerParams(vmem_limit_bytes=VMEM_BYTES),
        cost_estimate=cost(0, 4 * weights.size * 2),
        name="weights",
    )(plan, values, class_map, class_map, class_map)


def owner_of(me, chips, d, other):
    return lax.rem(me // 2 - d + chips, chips) * 2 + lax.rem(me + other, 2)


def product_of(pert, grad, member, level, c):
    total = None
    for v in range(grad.shape[1]):
        term = pert[member, level, v, :, span(c)].astype(F32) * grad[level, v, :, span(c)].astype(F32)
        total = term if total is None else total + term
    return total.astype(BF16)


def pack_owners_kernel(places, chips, d, plan, pert, near, far, tops, bottoms, top_rows, bottom_rows, offset):
    members, block = pert.shape[:2]
    capacity = tops.shape[0]
    at = pl.program_id(0)
    half = pl.num_programs(0) // 2
    owned = half * block

    @pl.when(at == 0)
    def _():
        offset[0] = 0

    def pack(grad, other, i):
        first = owner_of(plan[places.ME], chips, d, other) * owned + i * block
        for j in range(block):
            count = plan[places.steps + first + j]
            for m in range(members):
                off = jnp.minimum(offset[0], capacity)
                for c in range(top_rows.shape[0]):
                    part = product_of(pert, grad, m, j, c).astype(F32)
                    top_rows[c, pl.ds(off, ROWS), :] = part
                    bottom_rows[c, pl.ds(capacity - off, ROWS), :] = part
                offset[0] = off + count

    @pl.when(at < half)
    def _():
        pack(near, 0, at)

    @pl.when(at >= half)
    def _():
        pack(far, 1, at - half)

    @pl.when(at == 2 * half - 1)
    def _():
        for c in range(top_rows.shape[0]):
            tops[:, span(c)] = top_rows[c, :capacity, :].astype(BF16)
            bottoms[:, span(c)] = bottom_rows[c, ROWS:, :].astype(BF16)


def pack_owners(places, chips, d, plan, pert, near, far, block, capacity):
    members, _, variables, rows, cells = pert.shape
    blocks = near.shape[0] // block
    out = jax.ShapeDtypeStruct((capacity, cells), BF16)
    whole = pl.BlockSpec((capacity, cells), lambda i, plan: (0, 0))
    grad_block = (block, variables, rows, cells)

    def pert_place(i, plan):
        other = i // blocks
        return (0, owner_of(plan[places.ME], chips, d, other) * blocks + lax.rem(i, blocks), 0, 0, 0)

    return pl.pallas_call(
        functools.partial(pack_owners_kernel, places, chips, d),
        out_shape=(out, out),
        grid_spec=pltpu.PrefetchScalarGridSpec(
            num_scalar_prefetch=1,
            grid=(2 * blocks,),
            in_specs=[
                pl.BlockSpec((members,) + grad_block, pert_place),
                pl.BlockSpec(grad_block, lambda i, plan: (jnp.minimum(i, blocks - 1), 0, 0, 0)),
                pl.BlockSpec(grad_block, lambda i, plan: (jnp.maximum(i - blocks, 0), 0, 0, 0)),
            ],
            out_specs=[whole, whole],
            scratch_shapes=[
                pltpu.VMEM((cells // LANES, capacity + ROWS, LANES), F32),
                pltpu.VMEM((cells // LANES, capacity + ROWS, LANES), F32),
                pltpu.SMEM((1,), I32),
            ],
        ),
        compiler_params=pltpu.CompilerParams(vmem_limit_bytes=VMEM_BYTES),
        cost_estimate=cost(8 * near.size, 2 * near.size * 2 * (members + 1)),
    )(plan, pert, near, far)


def pack_members_kernel(places, chips, d, plan, pert, mate, grad, tops, bottoms, top_rows, bottom_rows, offset):
    members, block = pert.shape[:2]
    capacity = tops.shape[0]
    at = pl.program_id(0)
    owned = pl.num_programs(0) * block
    first = owner_of(plan[places.ME], chips, d, 0) * owned + at * block

    @pl.when(at == 0)
    def _():
        offset[0] = 0

    for j in range(block):
        count = plan[places.steps + first + j]
        for source in (pert, mate):
            for m in range(members):
                off = jnp.minimum(offset[0], capacity)
                for c in range(top_rows.shape[0]):
                    part = product_of(source, grad, m, j, c).astype(F32)
                    top_rows[c, pl.ds(off, ROWS), :] = part
                    bottom_rows[c, pl.ds(capacity - off, ROWS), :] = part
                offset[0] = off + count

    @pl.when(at == pl.num_programs(0) - 1)
    def _():
        for c in range(top_rows.shape[0]):
            tops[:, span(c)] = top_rows[c, :capacity, :].astype(BF16)
            bottoms[:, span(c)] = bottom_rows[c, ROWS:, :].astype(BF16)


def pack_members(places, chips, d, plan, pert, mate, grad, block, capacity):
    members, _, variables, rows, cells = pert.shape
    blocks = grad.shape[0] // block
    out = jax.ShapeDtypeStruct((capacity, cells), BF16)
    whole = pl.BlockSpec((capacity, cells), lambda i, plan: (0, 0))
    pert_block = (members, block, variables, rows, cells)

    def pert_place(i, plan):
        return (0, owner_of(plan[places.ME], chips, d, 0) * blocks + i, 0, 0, 0)

    return pl.pallas_call(
        functools.partial(pack_members_kernel, places, chips, d),
        out_shape=(out, out),
        grid_spec=pltpu.PrefetchScalarGridSpec(
            num_scalar_prefetch=1,
            grid=(blocks,),
            in_specs=[
                pl.BlockSpec(pert_block, pert_place),
                pl.BlockSpec(pert_block, lambda i, plan: (0, i, 0, 0, 0)),
                pl.BlockSpec(pert_block[1:], lambda i, plan: (i, 0, 0, 0)),
            ],
            out_specs=[whole, whole],
            scratch_shapes=[
                pltpu.VMEM((cells // LANES, capacity + ROWS, LANES), F32),
                pltpu.VMEM((cells // LANES, capacity + ROWS, LANES), F32),
                pltpu.SMEM((1,), I32),
            ],
        ),
        compiler_params=pltpu.CompilerParams(vmem_limit_bytes=VMEM_BYTES),
        cost_estimate=cost(16 * grad.size, grad.size * 2 * (2 * members + 1)),
    )(plan, pert, mate, grad)


def deep_product_kernel(places, chips, per_device, group, plan, *refs):
    perts, grads, out = refs[:group], refs[group:-1], refs[-1]
    members = perts[0].shape[0]
    count = len(grads) // group

    for u in range(group):
        k = pl.program_id(0) * group + u
        pert = perts[u]
        place = grad_place(places, chips, count, plan, k)[0]

        def form(grad):
            for m in range(members):
                spot = deep_place(k * members + m, out.shape[0], per_device)
                for c in range(pert.shape[-1] // LANES):
                    out[spot, :, span(c)] = product_of(pert, grad, m, 0, c)

        for g in range(count):
            pl.when(place == g)(functools.partial(form, grads[u * count + g]))


def grad_place(places, chips, count, plan, k):
    levels = places.ranks - places.steps
    owned = levels // count
    level = plan[places.deep + k]
    owner = level // owned
    shift = lax.rem(plan[places.ME] // 2 - owner // 2 + chips, chips)
    return 2 * shift + lax.rem(plan[places.ME] + owner, 2), lax.rem(level, owned)


def deep_products(places, chips, plan, pert, grads, top, per_device):
    members, _, variables, rows, cells = pert.shape
    group = 4 if top == 4 else 1

    def pert_spec(u):
        return pl.BlockSpec((members, 1, variables, rows, cells), lambda i, plan: (0, plan[places.deep + i * group + u], 0, 0, 0))

    def grad_spec(u, g):
        def where(i, plan):
            place, level = grad_place(places, chips, len(grads), plan, i * group + u)
            return (jnp.where(place == g, level, 0), 0, 0, 0)

        return pl.BlockSpec((1, variables, rows, cells), where)

    return pl.pallas_call(
        functools.partial(deep_product_kernel, places, chips, per_device, group),
        out_shape=jax.ShapeDtypeStruct((top * members, rows, cells), BF16),
        grid_spec=pltpu.PrefetchScalarGridSpec(
            num_scalar_prefetch=1,
            grid=(top // group,),
            in_specs=[pert_spec(u) for u in range(group)] + [grad_spec(u, g) for u in range(group) for g in range(len(grads))],
            out_specs=pl.BlockSpec((top * members, rows, cells), lambda i, plan: (0, 0, 0)),
        ),
        compiler_params=pltpu.CompilerParams(vmem_limit_bytes=VMEM_BYTES),
        cost_estimate=cost(top * members * rows * cells * 4, top * members * rows * cells * 8),
        name="deep_product",
    )(plan, *([pert] * group), *(list(grads) * group))


def deep_kernel(mine, plan, values, planes, class_map, out, field, keep, mix):
    at = pl.program_id(0)
    parts, _, rows, _ = planes.shape
    height = parts * rows
    tiles = field.shape[1]

    @pl.when(at == 0)
    def _():
        for c in range(tiles):
            field[0, c, :ROWS, :] = jnp.zeros((ROWS, LANES), F32)
            field[0, c, ROWS + height:, :] = jnp.zeros((ROWS, LANES), F32)
            store_weights(keep, mix, c, slice(0, height), diffusivity_of(class_map[:, span(c)], values))

    for p in range(parts):
        for c in range(tiles):
            field[0, c, ROWS + p * rows:ROWS + (p + 1) * rows, :] = planes[p, 0, :, span(c)].astype(F32)

    def step(i, carry):
        sweep(field, keep, mix, 0, ROWS, height)
        return carry

    lax.fori_loop(0, plan[mine + at], step, 0)
    for p in range(parts):
        for c in range(tiles):
            out[p, 0, :, span(c)] = field[0, c, ROWS + p * rows:ROWS + (p + 1) * rows, :].astype(BF16)


def deep_smooth(places, plan, planes, class_map, values):
    parts, per_device, rows, cells = planes.shape
    tiles = cells // LANES
    plane = pl.BlockSpec((parts, 1, rows, cells), lambda i: (0, i, 0, 0))
    return pl.pallas_call(
        functools.partial(deep_kernel, places.mine),
        out_shape=jax.ShapeDtypeStruct(planes.shape, BF16),
        grid=(per_device,),
        in_specs=[SMEM_SPEC, SMEM_SPEC, plane, VMEM_SPEC],
        out_specs=plane,
        scratch_shapes=[
            pltpu.VMEM((1, tiles, parts * rows + 2 * ROWS, LANES), F32),
            pltpu.VMEM((tiles, parts * rows, LANES), F32),
            pltpu.VMEM((tiles, parts * rows, LANES), F32),
        ],
        compiler_params=pltpu.CompilerParams(vmem_limit_bytes=VMEM_BYTES),
        cost_estimate=cost(150 * planes.size, planes.size * 4 + parts * rows * cells * 4),
        name="deep_smooth",
    )(plan, values, planes, class_map)


def deep_place(q, planes, per_device):
    devices = planes // per_device
    return lax.rem(q, devices) * per_device + q // devices


def smooth_kernel(places, chips, d, other, low, owned, top, per_device, with_mate, deep_count, with_variance, plan, pert, grad, below, above, keep, mix, *rest):
    extra, (out, below_rows, above_rows, field, offset) = rest[:-5], rest[-5:]
    perts = (pert,)
    if with_mate:
        perts, extra = (pert, extra[0]), extra[1:]
    deeps, extra = extra[:deep_count], extra[deep_count:]
    members, block = pert.shape[:2]
    sources = [(source, m) for source in perts for m in range(members)]
    capacity = below.shape[0]
    tiles = field.shape[1]
    at = pl.program_id(0)
    ahead = owner_of(plan[places.ME], chips, d, other) * owned

    @pl.when(at == 0)
    def _():
        start = jnp.int32(0)
        for owner, count in ([(0, owned)] if other else []) + [(other, low)]:
            base = places.steps + owner_of(plan[places.ME], chips, d, owner) * owned

            def add(j, total):
                return total + plan[base + j]

            start = lax.fori_loop(0, count, add, start)
        offset[0] = len(sources) * start
        for c in range(tiles):
            below_rows[c, :capacity, :] = below[:, span(c)].astype(F32)
            below_rows[c, capacity:, :] = jnp.zeros((ROWS, LANES), F32)
            above_rows[c, ROWS:, :] = above[:, span(c)].astype(F32)
            above_rows[c, :ROWS, :] = jnp.zeros((ROWS, LANES), F32)

    def emit(j, c, values):
        smooth = [value.astype(BF16).astype(F32) for value in values]
        for v in range(out.shape[1]):
            total = None
            for (source, m), value in zip(sources, smooth):
                term = source[m, j, v, :, span(c)].astype(F32) * value
                total = term if total is None else total + term
            if with_variance:
                total = total + extra[0][j, v, :, span(c)] * grad[j, v, :, span(c)].astype(F32)
            out[j, v, :, span(c)] = total.astype(out.dtype)

    def one_level(j, carry):
        level = ahead + low + at * block + j
        count = plan[places.steps + level]
        rank = plan[places.ranks + level]

        @pl.when(rank >= top)
        def _():
            for i, (source, m) in enumerate(sources):
                off = jnp.minimum(offset[0], capacity)
                for c in range(tiles):
                    field[i, c, :ROWS, :] = above_rows[c, pl.ds(capacity - off, ROWS), :]
                    field[i, c, ROWS:2 * ROWS, :] = product_of(source, grad, m, j, c).astype(F32)
                    field[i, c, 2 * ROWS:, :] = below_rows[c, pl.ds(off, ROWS), :]
                offset[0] = off + count

            def step(i, carry):
                for i in range(len(sources)):
                    sweep(field, keep, mix, i, ROWS - EDGE, ROWS + 2 * EDGE)
                return carry

            lax.fori_loop(1, count, step, 0)
            last = [diffuse_columns(field, keep, mix, i, ROWS, ROWS, EDGE) for i in range(len(sources))]
            for c, values in enumerate(zip(*last)):
                emit(j, c, values)

        @pl.when(rank < top)
        def _():
            for c in range(tiles):
                if deep_count > 0:
                    spots = [deep_place(rank * members + m, deeps[0].shape[0], per_device) for m in range(members)]
                    emit(j, c, [deep[spot, :, span(c)] for deep in deeps for spot in spots])
                else:
                    emit(j, c, [jnp.zeros((ROWS, LANES), F32)] * len(sources))

        return carry

    lax.fori_loop(0, block, one_level, 0)


def smooth_owner(places, chips, d, other, low, count, top, per_device, plan, pert, mate, grad, halos, keep, mix, deeps, variance, block, dtype):
    members, _, variables, rows, cells = pert.shape
    tiles = cells // LANES
    capacity = halos[0].shape[0]
    owned = grad.shape[0]
    mates = [] if mate is None else [mate]
    extra = [] if variance is None else [variance]
    kernel = functools.partial(
        smooth_kernel, places, chips, d, other, low, owned, top, per_device, mate is not None, len(deeps), variance is not None
    )

    def whole(x):
        return pl.BlockSpec(x.shape, lambda i, *refs: (0,) * x.ndim)

    def pert_place(i, plan):
        return (0, owner_of(plan[places.ME], chips, d, other) * (owned // block) + low // block + i, 0, 0, 0)

    def levels_from(start):
        return pl.BlockSpec((block, variables, rows, cells), lambda i, *refs: (start // block + i, 0, 0, 0))

    pert_block = (members, block, variables, rows, cells)
    return pl.pallas_call(
        kernel,
        out_shape=jax.ShapeDtypeStruct((count,) + grad.shape[1:], dtype),
        grid_spec=pltpu.PrefetchScalarGridSpec(
            num_scalar_prefetch=1,
            grid=(count // block,),
            in_specs=[pl.BlockSpec(pert_block, pert_place), levels_from(low)]
            + [whole(x) for x in (halos[0], halos[1], keep, mix)]
            + [pl.BlockSpec(pert_block, lambda i, plan: (0, low // block + i, 0, 0, 0)) for x in mates]
            + [whole(x) for x in deeps]
            + [levels_from(low) for x in extra],
            out_specs=levels_from(0),
            scratch_shapes=[
                pltpu.VMEM((tiles, capacity + ROWS, LANES), F32),
                pltpu.VMEM((tiles, capacity + ROWS, LANES), F32),
                pltpu.VMEM(((1 + len(mates)) * members, tiles, 3 * ROWS, LANES), F32),
                pltpu.SMEM((1,), I32),
            ],
        ),
        compiler_params=pltpu.CompilerParams(vmem_limit_bytes=VMEM_BYTES),
        cost_estimate=cost(100 * grad.size, grad.size * 2 * (members + 3)),
    )(plan, pert, grad, halos[0], halos[1], keep, mix, *mates, *deeps, *extra)


def final_kernel(places, top, per_device, owned, parts, plan, pert, near, part, deep, *rest):
    arrived, out = rest[:-1], rest[-1]
    members, block = pert.shape[:2]
    at = pl.program_id(0)
    steps = pl.num_programs(0)
    first = plan[places.ME] * owned + at * block

    def total_of(j, v, c):
        total = near[j, v, :, span(c)] + part[j, v, :, span(c)].astype(F32)
        for d in range(0, len(arrived), parts):
            value = arrived[d][j, v, :, span(c)]
            for p in range(1, parts):
                value = jnp.where(at >= p * steps // parts, arrived[d + p][j, v, :, span(c)], value)
            total = total + value.astype(F32)
        return total

    for j in range(block):
        rank = plan[places.ranks + first + j]
        for v in range(out.shape[1]):
            for c in range(out.shape[3] // LANES):
                out[j, v, :, span(c)] = total_of(j, v, c)

        @pl.when(rank < top)
        def _():
            for c in range(out.shape[3] // LANES):
                smooth = [deep[deep_place(rank * members + m, deep.shape[0], per_device), :, span(c)].astype(F32) for m in range(members)]
                for v in range(out.shape[1]):
                    total = out[j, v, :, span(c)]
                    for m in range(members):
                        total = total + pert[m, j, v, :, span(c)].astype(F32) * smooth[m]
                    out[j, v, :, span(c)] = total


def final_sum(places, top, per_device, parts, plan, pert, near, part, deep, arrived, block):
    members, _, variables, rows, cells = pert.shape
    owned = near.shape[0]
    steps = owned // block

    def levels_at(p):
        def where(i, plan):
            return (jnp.clip(i - p * steps // parts, 0, steps // parts - 1), 0, 0, 0)

        return pl.BlockSpec((block, variables, rows, cells), where)

    here = pl.BlockSpec((block, variables, rows, cells), lambda i, plan: (i, 0, 0, 0))
    return pl.pallas_call(
        functools.partial(final_kernel, places, top, per_device, owned, parts),
        out_shape=jax.ShapeDtypeStruct(near.shape, F32),
        grid_spec=pltpu.PrefetchScalarGridSpec(
            num_scalar_prefetch=1,
            grid=(steps,),
            in_specs=[
                pl.BlockSpec((members, block, variables, rows, cells), lambda i, plan: (0, plan[places.ME] * steps + i, 0, 0, 0)),
                here, here, pl.BlockSpec(deep.shape, lambda i, plan: (0, 0, 0)),
            ] + [levels_at(i % parts) for i in range(len(arrived))],
            out_specs=here,
        ),
        compiler_params=pltpu.CompilerParams(vmem_limit_bytes=VMEM_BYTES),
        cost_estimate=cost(4 * near.size, near.size * 12),
        name="final_sum",
    )(plan, pert, near, part, deep, *arrived)


def program(pert, gradient, variance, class_map, values, level_steps, top, capacities):
    members, levels, _, rows, cells = pert.shape
    mem_count = lax.axis_size("mem")
    tile_count = lax.axis_size("tile")
    owned = gradient.shape[0]
    chips = mem_count // 2
    per_device = top * members // tile_count
    places = Plan(levels, top, per_device)

    def hop(value, d):
        return lax.ppermute(value, "mem", [(i, ((i // 2 + d) % chips) * 2 + i % 2) for i in range(mem_count)])

    def swap(value):
        return lax.ppermute(value, "mem", [(i, i ^ 1) for i in range(mem_count)])

    south = [(i + 1, i) for i in range(tile_count - 1)]
    north = [(i, i + 1) for i in range(tile_count - 1)]

    grads = [gradient]
    for d in range(1, chips):
        grads.append(hop(gradient, d))
    me = lax.axis_index("mem")
    plan, fits = make_plan(places, top, per_device, owned, members, capacities, level_steps)
    keep, mix = make_weights(places, plan, values, class_map, rows)
    fits = fits[0] > 0
    mates = [None]
    for d in range(1, chips):
        mates.append(swap(lax.dynamic_slice_in_dim(pert, owner_of(me, chips, d, 1) * owned, owned, axis=1)))
    halos, both_grads = [], []
    for d in range(chips):
        other = swap(grads[d])
        both_grads += [grads[d], other]
        if top < levels:
            if d == 0:
                tops, bottoms = pack_owners(places, chips, d, plan, pert, gradient, other, min(8, owned), capacities[0])
            else:
                tops, bottoms = pack_members(places, chips, d, plan, pert, mates[d], grads[d], min(4, owned), capacities[1])
            below = lax.ppermute(tops, "tile", south)
            above = lax.ppermute(bottoms, "tile", north)
            halos.append((below, above))
        else:
            halos.append((jnp.zeros((16, cells), BF16),) * 2)

    deep = deep_products(places, chips, plan, pert, both_grads, top, per_device)
    deep = deep.reshape(tile_count, per_device, rows, cells)
    field = lax.all_to_all(deep, "tile", split_axis=0, concat_axis=0, tiled=True)
    field = deep_smooth(places, plan, field, class_map, values)
    deep = lax.all_to_all(field, "tile", split_axis=0, concat_axis=0, tiled=True).reshape(-1, rows, cells)
    deeps = (deep, swap(deep))

    def smooth(d, other, low, size, whole, var, dtype):
        return smooth_owner(
            places, chips, d, other, low, size, top, per_device, plan, pert, mates[d], both_grads[2 * d + other], halos[d], keep, mix,
            whole, var, min(2 if d else 4, size), dtype
        )

    near = smooth(0, 0, 0, owned, (), variance, F32)
    arrived = []
    size = owned // PARTS
    for d in range(1, chips):
        for p in range(PARTS):
            part = smooth(d, 0, p * size, size, deeps, None, BF16)
            arrived.append(hop(part, chips - d))
    part = smooth(0, 1, 0, owned, deeps[:1], None, BF16)
    part = swap(part)
    return fits, (plan, near, part, deep, arrived)


def finish(places, top, per_device, pert, sums):
    plan, near, part, deep, arrived = sums
    return final_sum(places, top, per_device, PARTS, plan, pert, near, part, deep, arrived, min(4, near.shape[0] // PARTS))


def shards(perturbations, gradient, static_variance, level_steps, class_map, class_diffusivity):
    members, levels = perturbations.shape[:2]
    owned = gradient.shape[0]
    top = lax.axis_size("tile") // members
    capacities = ((5 * members * owned + 7) // 8 * 8, (11 * members * owned // 2 + 7) // 8 * 8)
    operands = (perturbations, gradient, static_variance, class_map, class_diffusivity, level_steps)
    tiles = lax.axis_size("tile")
    fits, sums = program(*operands, top, capacities)

    def halo(sums, *operands):
        return finish(Plan(levels, top, top * members // tiles), top, top * members // tiles, operands[0], sums)

    def general(sums, *operands):
        per_device = levels * members // tiles
        return finish(Plan(levels, levels, per_device), levels, per_device, operands[0], program(*operands, levels, (0, 0))[1])

    return lax.cond(fits, halo, general, sums, *operands)


def solution(mesh):
    placed = (
        P("mem", None, None, "tile", None),
        P("mem", None, "tile", None),
        P("mem", None, "tile", None),
        P(),
        P(),
        P(),
    )
    return jax.shard_map(
        shards, mesh=mesh, in_specs=placed, out_specs=P("mem", None, "tile", None), check_vma=False
    )
```
